128 devices in a mesh: frag: 4 (over y), orb: 32 (over z, x, core).
Axes of the slice: x: 4, y: 4, z: 4, core: 2. Of those that a mesh axis runs over, the one named last changes fastest.
Arguments:
- orbitals: float32 [8, 128, 48, 2304], P('frag', 'orb'), may hold values from -6 to 6
- potential: float32 [24, 36864], P('frag', 'orb'), may hold values from -3 to 0
- ion_potential: float32 [24, 36864], P('frag', 'orb'), may hold values from -2 to 0
- core_density: float32 [24, 36864], P('frag', 'orb'), may hold values from 0.5 to 2
- frag_blocks: int32 [8, 3], replicated, may hold values from 0 to 23, as said below
- frag_signs: int32 [8], replicated, may hold values from -1 to 1, as said below
Outputs:
- filtered: float32 [8, 128, 48, 2304], P('frag', 'orb')
- new_potential: float32 [24, 36864], P('frag', 'orb')
The draws below stay inside these ranges and needn't reach their ends.
Inputs may be any that keep to these rules, and one draw needn't show every extreme that they name: `frag_blocks`: fragments g * 2 to (g + 1) * 2 - 1 form group g; block b belongs to owner b // 6. Among the 6 entries of one group no owner is named more than 3 times, and group g names owner (g + s) mod 4 exactly 3 times, for a shift s common to all groups. The first and the last block of every owner are named. `frag_signs`: each sign is +1 or -1.
All inputs are finite; a program needn't handle non-finite values.
Results may differ from the reference program's by a relative error of at most 0.0001.
Values sent between devices are 32-bit elements; how exact they have to be, the bound alone decides.
No kernel may reach another device: no remote copies, remote signals or barrier semaphores. Data moves between devices by JAX's collectives and lax.ppermute only.
A program may use at most 192 MiB of HBM per device.

```python
import math
import jax
import jax.numpy as jnp
from jax import lax

G = 48
FB = 3
ORBS = 128
ITERS = 2
FRAG_DEV = 2
FRAGS = 8
BLOCK = 36864
BLK_DEV = 6
NBLK = 24
CAP = 3
N_FRAG = 4


def draw_frag_blocks(key, part):
    entries = FRAG_DEV * FB
    others = entries - CAP
    subkeys = jax.random.split(jax.random.fold_in(key, 11), 4)
    shift_value = jax.random.randint(subkeys[0], (), 0, N_FRAG)
    busiest = (jnp.arange(N_FRAG, dtype=jnp.int32) + shift_value) % N_FRAG
    offsets = jax.random.randint(subkeys[1], (N_FRAG, others), 1, N_FRAG)
    owners = jnp.concatenate([jnp.broadcast_to(busiest[:, None], (N_FRAG, CAP)), (busiest[:, None] + offsets) % N_FRAG], axis=1)
    local_ids = jax.random.randint(subkeys[2], (N_FRAG, entries), 0, BLK_DEV)
    local_ids = local_ids.at[:, 0].set(BLK_DEV - 1)
    local_ids = local_ids.at[:, 1].set(0)
    scores = jax.random.randint(subkeys[3], (N_FRAG, entries), 0, 1048576) * entries + jnp.arange(entries, dtype=jnp.int32)[None, :]
    ordering = jnp.argsort(scores, axis=1)
    owners = jnp.take_along_axis(owners, ordering, axis=1)
    local_ids = jnp.take_along_axis(local_ids, ordering, axis=1)
    blocks = owners * BLK_DEV + local_ids
    return blocks.reshape(FRAGS, FB).astype(jnp.int32)


def draw_frag_signs(key, part):
    coins = jax.random.randint(jax.random.fold_in(key, 23), (FRAGS,), 0, 2)
    return (2 * coins - 1).astype(jnp.int32)


def levels(stream_key, dims, cuts, low, high):
    factor_of = 1.0
    for dim, parts in cuts:
        draws = jax.random.uniform(jax.random.fold_in(jax.random.fold_in(stream_key, 6), dim), (parts,), jnp.float32, low / len(cuts), high / len(cuts))
        factor_of = factor_of * jnp.repeat(jnp.exp(draws), dims[dim] // parts).reshape((-1,) + (1,) * (len(dims) - 1 - dim))
    return factor_of


def normal_values(key, shape, scale, most, cuts=(), kind=jnp.bfloat16):
    loudness = levels(key, shape, cuts, -0.22, 0.18) if cuts else 1.0
    values = jax.random.normal(key, shape, jnp.float32) * scale * loudness
    return jnp.minimum(jnp.maximum(values, -most), most).astype(kind)


def setup_inputs(seed: int = 0) -> dict:
    key_list = jax.random.split(jax.random.key(seed), 7)
    return {
        "orbitals": normal_values(key_list[0], (FRAGS, ORBS, G, G * G), 1.0, 6.0, ((0, 4), (1, 32)), jnp.float32),
        "potential": jnp.clip(-3.0 + 3.0 * jax.random.uniform(key_list[1], (NBLK, BLOCK), jnp.float32) ** levels(key_list[1], (NBLK, BLOCK), ((0, 4), (1, 32)), -0.2, 0.2), -3.0, 0.0),
        "ion_potential": jnp.clip(-2.0 + 2.0 * jax.random.uniform(key_list[2], (NBLK, BLOCK), jnp.float32) ** levels(key_list[2], (NBLK, BLOCK), ((0, 4), (1, 32)), -0.2, 0.2), -2.0, 0.0),
        "core_density": jnp.clip(jnp.exp(math.log(2.0) - 1.3862944 * jax.random.uniform(key_list[3], (NBLK, BLOCK), jnp.float32) ** levels(key_list[3], (NBLK, BLOCK), ((0, 4), (1, 32)), -0.2, 0.2)), 0.5, 2.0),
        "frag_blocks": draw_frag_blocks(jax.random.fold_in(key_list[6], 71), 0),
        "frag_signs": draw_frag_signs(jax.random.fold_in(key_list[6], 71), 0),
    }


SPACING = 0.5
FILTER_CENTER = 18.0
FILTER_HALF = 16.0
DENSITY_FLOOR = 0.25
EXCHANGE_COEF = 0.9847450218426965
NORM_EPS = 1e-06

def laplacian(values):
    side_cells = values.shape[-2]
    plane_cells = values.shape[-1]
    leading = [(0, 0)] * (values.ndim - 2)
    padded_x = jnp.pad(values, leading + [(2, 2), (0, 0)])
    nearest = padded_x[..., 1:side_cells + 1, :] + padded_x[..., 3:side_cells + 3, :]
    distant = padded_x[..., 0:side_cells, :] + padded_x[..., 4:side_cells + 4, :]
    padded_y = jnp.pad(values, leading + [(0, 0), (2 * side_cells, 2 * side_cells)])
    nearest = nearest + padded_y[..., side_cells:side_cells + plane_cells] + padded_y[..., 3 * side_cells:3 * side_cells + plane_cells]
    distant = distant + padded_y[..., 0:plane_cells] + padded_y[..., 4 * side_cells:4 * side_cells + plane_cells]
    padded_z = jnp.pad(values, leading + [(0, 0), (2, 2)])
    column = jnp.arange(plane_cells, dtype=jnp.int32) % side_cells
    nearest = nearest + jnp.where(column >= 1, padded_z[..., 1:1 + plane_cells], 0.0)
    nearest = nearest + jnp.where(column <= side_cells - 2, padded_z[..., 3:3 + plane_cells], 0.0)
    distant = distant + jnp.where(column >= 2, padded_z[..., 0:plane_cells], 0.0)
    distant = distant + jnp.where(column <= side_cells - 3, padded_z[..., 4:4 + plane_cells], 0.0)
    return (16.0 * nearest - distant - 90.0 * values) / 12.0

def hamiltonian(values, local_pot):
    return -0.5 / (SPACING * SPACING) * laplacian(values) + local_pot * values

def chebyshev(values, local_pot):
    previous = values
    current = (hamiltonian(values, local_pot) - FILTER_CENTER * values) / FILTER_HALF
    for degree in range(3):
        further = 2.0 * (hamiltonian(current, local_pot) - FILTER_CENTER * current) / FILTER_HALF - previous
        previous, current = (current, further)
    magnitude = jnp.sqrt(lax.optimization_barrier(jnp.mean(current * current, axis=(-2, -1), keepdims=True)) + NORM_EPS)
    return current / magnitude

def filter_fragment(operands):
    orbital_block, local_pot = operands
    result = chebyshev(orbital_block, local_pot)
    density = lax.optimization_barrier(jnp.sum(result * result, axis=0)) / ORBS
    return (result, density)

def reference(orbitals, potential, ion_potential, core_density, frag_blocks, frag_signs):
    entries = frag_blocks.reshape(-1).astype(jnp.int32)
    entry_signs = jnp.repeat(frag_signs, FB).astype(jnp.float32)
    current_pot = potential
    orbital_set = orbitals
    for iteration in range(ITERS):
        frag_pot = jnp.take(current_pot, entries, axis=0).reshape(FRAGS, 1, G, G * G)
        orbital_set, density = lax.map(filter_fragment, (orbital_set, frag_pot))
        pieces = density.reshape(FRAGS * FB, BLOCK) * entry_signs[:, None]
        total = core_density.at[entries].add(pieces)
        current_pot = ion_potential - EXCHANGE_COEF * jnp.cbrt(jnp.maximum(total, DENSITY_FLOOR))
    return (orbital_set, current_pot)
```

```python
import functools

import jax
import jax.numpy as jnp
import numpy as np
from jax import lax
from jax.experimental import pallas as pl
from jax.experimental.pallas import tpu as pltpu
from jax.sharding import PartitionSpec as P

G = 48
PLANE = G * G
FB = 3
ORBS = 128
N_FRAG = 4
SLOTS = 16
CHUNK = 16
LOADS = 6
XLOAD = G // LOADS
BIG = 40 << 20
ENT = 6
CELLS = 1152
ROWS = CELLS // 128
PIECE = ENT * ROWS
LOCAL = 8
COLS = 256
WIN = 512
STEPS = PLANE // COLS
PADDED = PLANE + 256
DENSITY_FLOOR = 0.25
EXCHANGE_COEF = 0.9847450218426965
NORM_EPS = 1e-6
F32 = jnp.float32
BF16 = jnp.bfloat16


def stencil_matrices():
    mats = np.zeros((3, WIN, COLS), np.float32)
    for phase in range(3):
        out = 768 + COLS * phase + np.arange(COLS)[None, :]
        src = 768 + COLS * phase - 128 + np.arange(WIN)[:, None]
        diff = np.abs(src - out)
        same = (src // G) == (out // G)
        mats[phase] = (
            np.where(diff == G, -16.0, 0.0)
            + np.where(diff == 2 * G, 1.0, 0.0)
            + np.where((diff == 1) & same, -16.0, 0.0)
            + np.where((diff == 2) & same, 1.0, 0.0)
        )
    return mats


def split(values):
    high = values.astype(BF16)
    low = (values - high.astype(F32)).astype(BF16)
    return high, low


def cols(start, size=128):
    return pl.ds(pl.multiple_of(start, 128), size)


def zero_planes(buf):
    buf[pl.ds(0, 2)] = jnp.zeros((2, LOCAL, PLANE), F32)
    buf[pl.ds(G + 2, 2)] = jnp.zeros((2, LOCAL, PLANE), F32)


def zero_margins(halves):
    for part in range(2):
        halves[:, pl.ds(part * PADDED, 128)] = jnp.zeros((G * LOCAL, 128), BF16)
        halves[:, pl.ds(part * PADDED + PLANE + 128, 128)] = jnp.zeros((G * LOCAL, 128), BF16)


def put_halves(halves, c, values):
    high, low = split(values.reshape(16, PLANE))
    rows = pl.ds(pl.multiple_of(16 * c, 16), 16)
    halves[rows, pl.ds(128, PLANE)] = high
    halves[rows, pl.ds(PADDED + 128, PLANE)] = low


def apply(kind, cur, prev, dst, wf, mats_ref, halves, halves_next, acc_even, acc_odd, sums):
    def product(n, c, acc):
        rows = pl.ds(CHUNK * LOCAL * c, CHUNK * LOCAL)
        mat = mats_ref[lax.rem(n, 3)]
        acc[rows, :] = jnp.dot(halves[rows, cols(COLS * n, WIN)], mat, preferred_element_type=F32) + jnp.dot(
            halves[rows, cols(PADDED + COLS * n, WIN)], mat, preferred_element_type=F32
        )

    def emit(n, c, acc):
        for t in range(COLS // 128):
            lane = cols(COLS * n + 128 * t)
            for d in range(CHUNK * c // 8, CHUNK * (c + 1) // 8):
                near = cur[pl.ds(8 * d, 12), :, lane]
                s1 = near[1:9] + near[3:11]
                s2 = near[0:8] + near[4:12]
                rows = pl.ds(64 * d, 64)
                plane = acc[rows, pl.ds(128 * t, 128)].reshape(8, LOCAL, 128)
                new = plane + s2 - 16.0 * s1
                here = pl.ds(8 * d + (0 if kind == "plain" else 2), 8)
                if kind == "plain":
                    dst[here, :, lane] = (0.5 / 48.0) * new
                    continue
                new = (1.0 / 48.0) * new + wf[pl.ds(8 * d, 8), :, lane] * near[2:10]
                new = new - prev[pl.ds(8 * d + 2, 8), :, lane]
                dst[here, :, lane] = new
                if kind == "last":
                    sums[...] += jnp.sum(new * new, axis=0)
                else:
                    high, low = split(new.reshape(64, 128))
                    halves_next[rows, cols(COLS * n + 128 * t + 128)] = high
                    halves_next[rows, cols(PADDED + COLS * n + 128 * t + 128)] = low

    parts = G // CHUNK
    for c in range(parts):
        product(0, c, acc_even)

    def body(i, carry):
        for c in range(parts):
            product(2 * i + 1, c, acc_odd)
            emit(2 * i, c, acc_even)
        for c in range(parts):
            product(2 * i + 2, c, acc_even)
            emit(2 * i + 1, c, acc_odd)
        return carry

    lax.fori_loop(0, STEPS // 2, body, 0)
    for c in range(parts):
        emit(STEPS - 1, c, acc_even)


def prepare_kernel(first, source, *refs):
    if first:
        mats_ref, field_hbm, plain_hbm, field, plain, hl, acc0, acc1, sem = refs
        loads = [pltpu.make_async_copy(source.at[o], field.at[pl.ds(2, G), o, :], sem.at[o]) for o in range(LOCAL)]
    else:
        scale_ref, mats_ref, field_hbm, plain_hbm, field, plain, hl, acc0, acc1, sem = refs
        loads = [pltpu.make_async_copy(source, field.at[pl.ds(2, G)], sem.at[0])]
    for load in loads:
        load.start()
    zero_planes(field)
    zero_margins(hl)
    for load in loads:
        load.wait()
    scale = None if first else jnp.broadcast_to(scale_ref[:, 0:1], (LOCAL, PLANE))

    def body(c, scale):
        x = pl.ds(2 + 2 * c, 2)
        values = field[x]
        if not first:
            values = values * scale[None]
            field[x] = values
        put_halves(hl, c, values)
        return scale

    lax.fori_loop(0, G // 2, body, scale)
    stores = [
        pltpu.make_async_copy(field.at[pl.ds(2, G)], field_hbm, sem.at[0]),
        pltpu.make_async_copy(plain, plain_hbm, sem.at[1]),
    ]
    stores[0].start()
    apply("plain", field, None, plain, None, mats_ref, hl, None, acc0, acc1, None)
    stores[1].start()
    for store in stores:
        store.wait()


def filter_kernel(field_hbm, plain_hbm, mine_ref, other_ref, mats_ref, raw_hbm, scale_ref, dmine_ref, dother_ref,
                  ya, yb, wf, hl0, hl1, acc0, acc1, sums, sem):
    core = lax.axis_index("orb") % 2
    loads = []
    for p in range(LOADS):
        x = pl.ds(XLOAD * p, XLOAD)
        inner = pl.ds(2 + XLOAD * p, XLOAD)
        loads.append(pltpu.make_async_copy(field_hbm.at[x], ya.at[inner], sem.at[2 * p]))
        loads.append(pltpu.make_async_copy(plain_hbm.at[x], yb.at[inner], sem.at[2 * p + 1]))
    for load in loads:
        load.start()
    upper = lax.broadcasted_iota(jnp.int32, (LOCAL, 128), 0) >= LOCAL // 2

    def build(row, carry):
        for ref, half in ((mine_ref, core), (other_ref, 1 - core)):
            for b in range(FB):
                tiles = []
                for q in range(ROWS):
                    v0 = ref[row, pl.ds(b * ROWS + q, 1), :]
                    v1 = ref[row, pl.ds((FB + b) * ROWS + q, 1), :]
                    v = jnp.where(upper, jnp.broadcast_to(v1, (LOCAL, 128)), jnp.broadcast_to(v0, (LOCAL, 128)))
                    tiles.append(v * 0.125 - 0.375)
                wf[16 * b + row, :, cols(half * CELLS, CELLS)] = jnp.concatenate(tiles, axis=1)
        return carry

    lax.fori_loop(0, SLOTS, build, 0)
    zero_planes(ya)
    zero_planes(yb)
    zero_margins(hl0)
    zero_margins(hl1)
    sums[...] = jnp.zeros((LOCAL, 128), F32)

    def start(c, carry):
        x = pl.ds(2 + 2 * c, 2)
        value = yb[x] + 0.5 * (wf[pl.ds(2 * c, 2)] * ya[x])
        yb[x] = value
        put_halves(hl0, c, value)
        return carry

    for p in range(LOADS):
        loads[2 * p].wait()
        loads[2 * p + 1].wait()
        lax.fori_loop(p * XLOAD // 2, (p + 1) * XLOAD // 2, start, 0)
    apply("middle", yb, ya, ya, wf, mats_ref, hl0, hl1, acc0, acc1, sums)
    apply("middle", ya, yb, yb, wf, mats_ref, hl1, hl0, acc0, acc1, sums)
    apply("last", yb, ya, ya, wf, mats_ref, hl0, None, acc0, acc1, sums)
    store = pltpu.make_async_copy(ya.at[pl.ds(2, G)], raw_hbm, sem.at[0])
    store.start()
    mean = jnp.sum(sums[...], axis=1, keepdims=True) * (1.0 / (G * PLANE))
    inverse = 1.0 / jnp.sqrt(mean + NORM_EPS)
    scale_ref[...] = jnp.broadcast_to(inverse, (LOCAL, 128))

    def finish(row, scale):
        for ref, half in ((dmine_ref, core), (dother_ref, 1 - core)):
            for b in range(FB):
                value = ya[2 + 16 * b + row, :, cols(half * CELLS, CELLS)] * scale
                value = value * value
                value = value + pltpu.roll(value, 1, 0)
                value = value + pltpu.roll(value, 2, 0)
                for q in range(ROWS):
                    ref[row, pl.ds(b * ROWS + q, 1), :] = value[3:4, 128 * q : 128 * q + 128]
                    ref[row, pl.ds((FB + b) * ROWS + q, 1), :] = value[7:8, 128 * q : 128 * q + 128]
            ref[row, pl.ds(PIECE, 2), :] = jnp.zeros((2, 128), F32)
        return scale

    lax.fori_loop(0, SLOTS, finish, jnp.broadcast_to(inverse, (LOCAL, CELLS)))
    store.wait()


def write_kernel(raw_hbm, scale_ref, out_ref, buf, sem):
    loads = []
    for b in range(FB):
        x = pl.ds(16 * b, 16)
        loads.append(pltpu.make_async_copy(raw_hbm.at[x], buf.at[x], sem.at[FB * LOCAL + b]))
        loads[-1].start()
    stores = []
    scale = jnp.broadcast_to(scale_ref[:, 0:1], (LOCAL, PLANE))
    for b in range(FB):
        loads[b].wait()

        def body(c, scale):
            x = pl.ds(16 * b + 2 * c, 2)
            buf[x] = buf[x] * scale[None]
            return scale

        lax.fori_loop(0, 8, body, scale)
        x = pl.ds(16 * b, 16)
        for o in range(LOCAL):
            stores.append(pltpu.make_async_copy(buf.at[x, o, :], out_ref.at[o, x], sem.at[b * LOCAL + o]))
            stores[-1].start()
    for store in stores:
        store.wait()


VMEM_SPEC = pl.BlockSpec(memory_space=pltpu.VMEM)
SMEM_SPEC = pl.BlockSpec(memory_space=pltpu.SMEM)
HBM_SPEC = pl.BlockSpec(memory_space=pltpu.HBM)
PLANES = pltpu.VMEM((G + 4, LOCAL, PLANE), F32)
RAW = jax.ShapeDtypeStruct((G, LOCAL, PLANE), F32)
RAW_HBM = pltpu.HBM((G, LOCAL, PLANE), F32)
SCALE = jax.ShapeDtypeStruct((LOCAL, 128), F32)
SPREAD = jax.ShapeDtypeStruct((SLOTS, PIECE + 2, 128), F32)
HALVES = pltpu.VMEM((G * LOCAL, 2 * PADDED), BF16)
ACC = pltpu.VMEM((G * LOCAL, COLS), F32)
MATS = (3, WIN, COLS)


def in_hbm(value):
    return pltpu.with_memory_space_constraint(value, pltpu.HBM)


def prepare_call(first, source, mats):
    return pl.pallas_call(
        functools.partial(prepare_kernel, first),
        out_shape=(RAW_HBM, RAW_HBM),
        in_specs=[HBM_SPEC] + [VMEM_SPEC] * len(source),
        out_specs=(HBM_SPEC, HBM_SPEC),
        scratch_shapes=[PLANES, pltpu.VMEM(RAW.shape, F32), HALVES, ACC, ACC, pltpu.SemaphoreType.DMA((LOCAL,))],
        name="prepare_first" if first else "prepare_next",
        cost_estimate=pl.CostEstimate(flops=2 * 10**9, bytes_accessed=11 * 10**6, transcendentals=0),
        compiler_params=pltpu.CompilerParams(vmem_limit_bytes=BIG),
    )(in_hbm(source[0]), *source[1:], mats)


def filter_call(field, plain, mine, other, mats):
    return pl.pallas_call(
        filter_kernel,
        out_shape=(RAW_HBM, SCALE, SPREAD, SPREAD),
        in_specs=[HBM_SPEC] * 2 + [VMEM_SPEC] * 3,
        out_specs=(HBM_SPEC,) + (VMEM_SPEC,) * 3,
        scratch_shapes=[
            PLANES,
            PLANES,
            pltpu.VMEM(RAW.shape, F32),
            HALVES,
            HALVES,
            ACC,
            ACC,
            pltpu.VMEM((LOCAL, 128), F32),
            pltpu.SemaphoreType.DMA((2 * LOADS,)),
        ],
        name="filter",
        cost_estimate=pl.CostEstimate(flops=8 * 10**9, bytes_accessed=14 * 10**6, transcendentals=0),
        compiler_params=pltpu.CompilerParams(vmem_limit_bytes=BIG),
    )(in_hbm(field), in_hbm(plain), mine, other, mats)


def write_call(raw, scale):
    return pl.pallas_call(
        write_kernel,
        out_shape=pltpu.HBM((LOCAL, G, PLANE), F32),
        in_specs=[HBM_SPEC, VMEM_SPEC],
        out_specs=HBM_SPEC,
        scratch_shapes=[pltpu.VMEM(RAW.shape, F32), pltpu.SemaphoreType.DMA((FB * LOCAL + FB,))],
        name="write",
        cost_estimate=pl.CostEstimate(flops=10**6, bytes_accessed=11 * 10**6, transcendentals=0),
        compiler_params=pltpu.CompilerParams(vmem_limit_bytes=BIG),
    )(in_hbm(raw), scale)


def entry(blocks_ref, group, e):
    return blocks_ref[e % FB, 2 * group + e // FB]


def select_kernel(count, blocks_ref, *refs):
    group = lax.axis_index("frag")
    ins, outs, rows = refs[:4], refs[4:-1], refs[-1]
    for k in range(count):
        for s in range(N_FRAG):
            for e in range(ENT):
                for q in range(ROWS):
                    rows[k, s * ENT + e, pl.ds(q, 1), :] = ins[s][k, pl.ds(e, 1), pl.ds(128 * q, 128)]
    for k in range(count):
        for e in range(ENT):
            block = entry(blocks_ref, group, e)
            place = lax.rem(group - block // ENT + N_FRAG, N_FRAG) * ENT + lax.rem(block, ENT)
            outs[k][pl.ds(e * ROWS, ROWS), :] = rows[k, place]
            outs[count + k][pl.ds(e * ROWS, ROWS), :] = rows[k, e]


def select_call(blocks, arrays):
    count = arrays[0].shape[0]
    piece = jax.ShapeDtypeStruct((PIECE, 128), F32)
    out_shape = (piece,) * (2 * count)
    return pl.pallas_call(
        functools.partial(select_kernel, count),
        out_shape=out_shape,
        in_specs=[SMEM_SPEC] + [VMEM_SPEC] * 4,
        out_specs=(VMEM_SPEC,) * (2 * count),
        scratch_shapes=[pltpu.VMEM((count, N_FRAG * ENT, ROWS, 128), F32)],
        name=f"select{count}",
        compiler_params=pltpu.CompilerParams(vmem_limit_bytes=8 << 20),
    )(blocks, *arrays)


def place_kernel(blocks_hbm, p0_hbm, p1, p2, p3, out_ref, rows, p0, blocks_ref, sem):
    loads = [pltpu.make_async_copy(blocks_hbm, blocks_ref, sem.at[0]), pltpu.make_async_copy(p0_hbm, p0, sem.at[1])]
    for load in loads:
        load.start()
    group = lax.axis_index("frag")
    for s, ref in ((1, p1), (2, p2), (3, p3), (0, p0)):
        if s == 0:
            for load in loads:
                load.wait()
        for e in range(ENT):
            for q in range(ROWS):
                rows[s * ENT + e, pl.ds(q, 1), :] = ref[pl.ds(e, 1), pl.ds(128 * q, 128)]
    tail = jnp.zeros((2, 128), F32)
    for e in range(ENT):
        block = entry(blocks_ref, group, e)
        place = lax.rem(group - block // ENT + N_FRAG, N_FRAG) * ENT + lax.rem(block, ENT)
        value = rows[place]
        for slot in range(SLOTS):
            out_ref[slot, pl.ds(e * ROWS, ROWS), :] = value
    for slot in range(SLOTS):
        out_ref[slot, pl.ds(PIECE, 2), :] = tail


def place_call(blocks, pots):
    return pl.pallas_call(
        place_kernel,
        out_shape=SPREAD,
        in_specs=[HBM_SPEC] * 2 + [VMEM_SPEC] * 3,
        out_specs=VMEM_SPEC,
        scratch_shapes=[
            pltpu.VMEM((N_FRAG * ENT, ROWS, 128), F32),
            pltpu.VMEM((ENT, CELLS), F32),
            pltpu.SMEM((FB, 2 * N_FRAG), jnp.int32),
            pltpu.SemaphoreType.DMA((2,)),
        ],
        name="place",
        compiler_params=pltpu.CompilerParams(vmem_limit_bytes=8 << 20),
    )(in_hbm(blocks), in_hbm(pots[0]), *pots[1:])


def update_kernel(final, blocks_ref, signs_ref, core_ref, ion_ref, d0, d1, d2, d3, out_ref):
    group = lax.axis_index("frag")
    seen = []
    for s, d in enumerate((d0, d1, d2, d3)):
        source = lax.rem(group - s + N_FRAG, N_FRAG)
        for k in range(ENT):
            sign = jnp.where(signs_ref[2 * source + k // FB] > 0, 1.0 / ORBS, -1.0 / ORBS)
            seen.append((entry(blocks_ref, source, k), sign.astype(F32), d[pl.ds(k * ROWS, ROWS), :]))
    for e in range(ENT):
        mine = group * ENT + e if final else entry(blocks_ref, group, e)
        total = core_ref[pl.ds(e * ROWS, ROWS), :]
        for block, sign, density in seen:
            total = total + jnp.where(block == mine, sign, jnp.float32(0.0)) * density
        total = jnp.maximum(total, DENSITY_FLOOR)
        root = jnp.exp(jnp.log(total) * (1.0 / 3.0))
        root = root - (root * root * root - total) / (3.0 * root * root)
        value = ion_ref[pl.ds(e * ROWS, ROWS), :] - EXCHANGE_COEF * root
        if final:
            for q in range(ROWS):
                out_ref[pl.ds(e, 1), pl.ds(128 * q, 128)] = value[q : q + 1]
        else:
            for slot in range(SLOTS):
                out_ref[slot, pl.ds(e * ROWS, ROWS), :] = value
    if not final:
        for slot in range(SLOTS):
            out_ref[slot, pl.ds(PIECE, 2), :] = jnp.zeros((2, 128), F32)


def update_call(final, blocks, signs, core, ion, densities):
    return pl.pallas_call(
        functools.partial(update_kernel, final),
        out_shape=jax.ShapeDtypeStruct((ENT, CELLS), F32) if final else SPREAD,
        in_specs=[SMEM_SPEC] * 2 + [VMEM_SPEC] * 6,
        out_specs=VMEM_SPEC,
        name="update_last" if final else "update_first",
        compiler_params=pltpu.CompilerParams(vmem_limit_bytes=8 << 20),
    )(blocks, signs, core, ion, *densities)


def frag_all(value):
    return [value] + [
        lax.ppermute(value, "frag", [(g, (g + s) % N_FRAG) for g in range(N_FRAG)]) for s in (1, 2, 3)
    ]


def core_swap(value):
    return lax.ppermute(value, "orb", [(i, i ^ 1) for i in range(2 * SLOTS)])


def plane_exchange(value):
    groups = [[2 * i + c for i in range(SLOTS)] for c in range(2)]
    return lax.all_to_all(value, "orb", 0, 0, axis_index_groups=groups, tiled=True)


def shards(orbitals, potential, ion_potential, core_density, frag_blocks, frag_signs):
    blocks = frag_blocks.T
    mats = jnp.asarray(stencil_matrices(), BF16)

    pots = frag_all(potential)
    spread, source = lax.optimization_barrier((place_call(blocks, pots), orbitals.reshape(LOCAL, G, PLANE)))
    near = plane_exchange(spread)
    field, plain = prepare_call(True, (source,), mats)
    near, field = lax.optimization_barrier((near, field))
    statics = frag_all(jnp.stack([core_density, ion_potential]))
    raw, scale, mine, other = filter_call(field, plain, near, core_swap(near), mats)
    cores, ions, own_core, own_ion = select_call(blocks, statics)

    density, raw = lax.optimization_barrier((mine + core_swap(other), raw))
    density = plane_exchange(density)
    field, plain = prepare_call(False, (raw, scale), mats)
    density, field = lax.optimization_barrier((density, field))
    densities = frag_all(jnp.sum(density, axis=0))
    near = plane_exchange(update_call(False, blocks, frag_signs, cores, ions, densities))
    raw, scale, mine, other = filter_call(field, plain, near, core_swap(near), mats)

    density, raw = lax.optimization_barrier((mine + core_swap(other), raw))
    density = plane_exchange(density)
    filtered = write_call(raw, scale)
    density, filtered = lax.optimization_barrier((density, filtered))
    densities = frag_all(jnp.sum(density, axis=0))
    new_potential = update_call(True, blocks, frag_signs, own_core, own_ion, densities)
    return (filtered.reshape(orbitals.shape), new_potential)


def solution(mesh):
    in_specs = (
        P("frag", "orb", None, None),
        P("frag", "orb"),
        P("frag", "orb"),
        P("frag", "orb"),
        P(),
        P(),
    )
    out_specs = (P("frag", "orb", None, None), P("frag", "orb"))
    return jax.shard_map(shards, mesh=mesh, in_specs=in_specs, out_specs=out_specs, check_vma=False)
```

```python
import functools

import jax
import jax.numpy as jnp
import numpy as np
from jax import lax
from jax.experimental import pallas as pl
from jax.experimental.pallas import tpu as pltpu
from jax.sharding import PartitionSpec as P

G = 48
PLANE = G * G
FB = 3
ORBS = 128
N_FRAG = 4
SLOTS = 16
BAND = 64
BANDS = 6
UNROLL = 4
LOADS = 6
XLOAD = G // LOADS
BIG = 40 << 20
ENT = 6
CELLS = 1152
ROWS = CELLS // 128
PIECE = ENT * ROWS
LOCAL = 8
COLS = 256
WIN = 512
STEPS = PLANE // COLS
TILES = PLANE // 128 + 2
DENSITY_FLOOR = 0.25
EXCHANGE_COEF = 0.9847450218426965
NORM_EPS = 1e-6
F32 = jnp.float32
BF16 = jnp.bfloat16


def stencil_matrices():
    mats = np.zeros((3, WIN, COLS), np.float32)
    for phase in range(3):
        out = 768 + COLS * phase + np.arange(COLS)[None, :]
        src = 768 + COLS * phase - 128 + np.arange(WIN)[:, None]
        diff = np.abs(src - out)
        same = (src // G) == (out // G)
        mats[phase] = (
            np.where(diff == G, -16.0, 0.0)
            + np.where(diff == 2 * G, 1.0, 0.0)
            + np.where((diff == 1) & same, -16.0, 0.0)
            + np.where((diff == 2) & same, 1.0, 0.0)
        )
    return mats


def split(values):
    high = values.astype(BF16)
    low = (values - high.astype(F32)).astype(BF16)
    return high, low


def cols(start, size=128):
    return pl.ds(pl.multiple_of(start, 128), size)


def zero_planes(buf):
    buf[pl.ds(0, 2)] = jnp.zeros((2, LOCAL, PLANE), F32)
    buf[pl.ds(G + 2, 2)] = jnp.zeros((2, LOCAL, PLANE), F32)


def zero_margins(halves):
    for part in range(2):
        halves[part * TILES] = jnp.zeros((G * LOCAL, 128), BF16)
        halves[part * TILES + TILES - 1] = jnp.zeros((G * LOCAL, 128), BF16)


def put_halves(halves, c, values):
    rows = pl.ds(pl.multiple_of(16 * c, 16), 16)
    for j in range(TILES - 2):
        high, low = split(values[:, :, 128 * j : 128 * j + 128].reshape(16, 128))
        halves[1 + j, rows, :] = high
        halves[TILES + 1 + j, rows, :] = low


def run_chain(apps, mats_ref):
    def scoped(*accs):
        def acc(parity, unit, i):
            return accs[(2 * parity + unit) * BANDS + i]

        def push(n, parity, unit):
            mat = jnp.concatenate([mats_ref[lax.rem(n, 3), t, pl.ds(COLS * unit, COLS), :] for t in range(2)], axis=1)
            pltpu.matmul_push_rhs(mat, staging_register=parity, mxu_index=unit)

        def feed(app, n, parity, i):
            halves = app[5]
            rows = pl.ds(BAND * i, BAND)
            for unit in range(2):
                high, low = (
                    jnp.concatenate([halves[part * TILES + 2 * (n + unit) + t, rows, :] for t in range(2)], axis=1)
                    for part in range(2)
                )
                pltpu.matmul_acc_lhs(acc(parity, unit, i), high, load_staged_rhs=parity if i == 0 else None)
                pltpu.matmul_acc_lhs(acc(parity, unit, i), low)
                if i == BANDS - 2 + unit:
                    push(n + 1, 1 - parity, unit)

        def emit(app, n, parity, i):
            kind, cur, prev, dst, wf, _, halves_next, sums, done = app
            rows = pl.ds(BAND * i, BAND)
            values = pltpu.matmul_pop(acc(parity, 0, i)) + pltpu.matmul_pop(acc(parity, 1, i))
            for t in range(COLS // 128):
                lane = cols(COLS * n + 128 * t)
                near = cur[pl.ds(8 * i, 12), :, lane]
                s1 = near[1:9] + near[3:11]
                s2 = near[0:8] + near[4:12]
                plane = values[:, 128 * t : 128 * t + 128].reshape(8, LOCAL, 128)
                new = plane + s2 - 16.0 * s1
                here = pl.ds(8 * i + (0 if kind == "plain" else 2), 8)
                if kind == "plain":
                    dst[here, :, lane] = (0.5 / 48.0) * new
                    continue
                new = (1.0 / 48.0) * new + wf[pl.ds(8 * i, 8), :, lane] * near[2:10]
                new = new - prev[pl.ds(8 * i + 2, 8), :, lane]
                dst[here, :, lane] = new
                if kind == "last":
                    sums[...] += jnp.sum(new * new, axis=0)
                else:
                    high, low = split(new.reshape(BAND, 128))
                    halves_next[2 * n + t + 1, rows, :] = high
                    halves_next[TILES + 2 * n + t + 1, rows, :] = low
            if done is not None and i == BANDS - 1:
                done(n)

        for unit in range(2):
            push(0, 0, unit)
        for i in range(BANDS):
            feed(apps[0], 0, 0, i)
        for number, app in enumerate(apps):

            def body(j, carry):
                for u in range(UNROLL):
                    for i in range(BANDS):
                        feed(app, UNROLL * j + u + 1, (number + u + 1) % 2, i)
                        emit(app, UNROLL * j + u, (number + u) % 2, i)
                return carry

            lax.fori_loop(0, STEPS // UNROLL, body, 0)
            for i in range(BANDS):
                if number + 1 < len(apps):
                    feed(apps[number + 1], 0, (number + 1) % 2, i)
                emit(app, STEPS - 1, number % 2, i)
        rest = len(apps) % 2
        for unit in range(2):
            pltpu.matmul_acc_lhs(acc(rest, unit, 0), jnp.zeros((BAND, COLS), BF16), load_staged_rhs=rest)
            pltpu.matmul_pop(acc(rest, unit, 0))

    pl.run_scoped(
        scoped,
        *[pltpu.ACC(unit)((BAND, COLS), F32) for _ in range(2) for unit in range(2) for _ in range(BANDS)],
    )


def prepare_kernel(first, source, *refs):
    if first:
        mats_ref, field_hbm, plain_hbm, field, plain, hl, sem = refs
    else:
        scale_ref, mats_ref, field_hbm, plain_hbm, field, plain, hl, sem = refs
    loads = []
    for p in range(FB):
        inner = pl.ds(2 + 16 * p, 16)
        x = pl.ds(16 * p, 16)
        if first:
            loads.append(
                [
                    pltpu.make_async_copy(source.at[o, x], field.at[inner, o, :], sem.at[LOCAL * p + o])
                    for o in range(LOCAL)
                ]
            )
        else:
            loads.append([pltpu.make_async_copy(source.at[x], field.at[inner], sem.at[LOCAL * p])])
        for load in loads[-1]:
            load.start()
    zero_planes(field)
    zero_margins(hl)
    scale = None if first else jnp.broadcast_to(scale_ref[:, 0:1], (LOCAL, PLANE))

    def body(c, scale):
        x = pl.ds(2 + 2 * c, 2)
        values = field[x]
        if not first:
            values = values * scale[None]
            field[x] = values
        put_halves(hl, c, values)
        return scale

    stores = []
    for p in range(FB):
        for load in loads[p]:
            load.wait()
        lax.fori_loop(8 * p, 8 * p + 8, body, scale)
        stores.append(
            pltpu.make_async_copy(
                field.at[pl.ds(2 + 16 * p, 16)], field_hbm.at[pl.ds(16 * p, 16)], sem.at[FB * LOCAL + p]
            )
        )
        stores[-1].start()

    def column(n):
        lane = cols(COLS * n, COLS)
        return pltpu.make_async_copy(plain.at[:, :, lane], plain_hbm.at[:, :, lane], sem.at[FB * (LOCAL + 1) + n])

    run_chain([("plain", field, None, plain, None, hl, None, None, lambda n: column(n).start())], mats_ref)
    for store in stores:
        store.wait()
    for n in range(STEPS):
        column(n).wait()


def filter_kernel(field_hbm, plain_hbm, mine_ref, other_ref, mats_ref, raw_hbm, scale_ref, dmine_ref, dother_ref,
                  ya, yb, wf, hl0, hl1, sums, sem):
    core = lax.axis_index("orb") % 2
    loads = []
    for p in range(LOADS):
        x = pl.ds(XLOAD * p, XLOAD)
        inner = pl.ds(2 + XLOAD * p, XLOAD)
        loads.append(pltpu.make_async_copy(field_hbm.at[x], ya.at[inner], sem.at[2 * p]))
        loads.append(pltpu.make_async_copy(plain_hbm.at[x], yb.at[inner], sem.at[2 * p + 1]))
    for load in loads:
        load.start()
    upper = lax.broadcasted_iota(jnp.int32, (LOCAL, 128), 0) >= LOCAL // 2

    def build(row, carry):
        for ref, half in ((mine_ref, core), (other_ref, 1 - core)):
            for b in range(FB):
                tiles = []
                for q in range(ROWS):
                    v0 = ref[row, pl.ds(b * ROWS + q, 1), :]
                    v1 = ref[row, pl.ds((FB + b) * ROWS + q, 1), :]
                    v = jnp.where(upper, jnp.broadcast_to(v1, (LOCAL, 128)), jnp.broadcast_to(v0, (LOCAL, 128)))
                    tiles.append(v * 0.125 - 0.375)
                wf[16 * b + row, :, cols(half * CELLS, CELLS)] = jnp.concatenate(tiles, axis=1)
        return carry

    lax.fori_loop(0, SLOTS, build, 0, unroll=2)
    zero_planes(ya)
    zero_planes(yb)
    zero_margins(hl0)
    zero_margins(hl1)
    sums[...] = jnp.zeros((LOCAL, 128), F32)

    def start(c, carry):
        x = pl.ds(2 + 2 * c, 2)
        value = yb[x] + 0.5 * (wf[pl.ds(2 * c, 2)] * ya[x])
        yb[x] = value
        put_halves(hl0, c, value)
        return carry

    for p in range(LOADS):
        loads[2 * p].wait()
        loads[2 * p + 1].wait()
        lax.fori_loop(p * XLOAD // 2, (p + 1) * XLOAD // 2, start, 0)
    run_chain(
        [
            ("middle", yb, ya, ya, wf, hl0, hl1, sums, None),
            ("middle", ya, yb, yb, wf, hl1, hl0, sums, None),
            ("last", yb, ya, ya, wf, hl0, None, sums, None),
        ],
        mats_ref,
    )
    store = pltpu.make_async_copy(ya.at[pl.ds(2, G)], raw_hbm, sem.at[0])
    store.start()
    mean = jnp.sum(sums[...], axis=1, keepdims=True) * (1.0 / (G * PLANE))
    inverse = 1.0 / jnp.sqrt(mean + NORM_EPS)
    scale_ref[...] = jnp.broadcast_to(inverse, (LOCAL, 128))

    def finish(row, scale):
        for ref, half in ((dmine_ref, core), (dother_ref, 1 - core)):
            for b in range(FB):
                value = ya[2 + 16 * b + row, :, cols(half * CELLS, CELLS)] * scale
                value = value * value
                value = value + pltpu.roll(value, 1, 0)
                value = value + pltpu.roll(value, 2, 0)
                for q in range(ROWS):
                    ref[row, pl.ds(b * ROWS + q, 1), :] = value[3:4, 128 * q : 128 * q + 128]
                    ref[row, pl.ds((FB + b) * ROWS + q, 1), :] = value[7:8, 128 * q : 128 * q + 128]
            ref[row, pl.ds(PIECE, 2), :] = jnp.zeros((2, 128), F32)
        return scale

    lax.fori_loop(0, SLOTS, finish, jnp.broadcast_to(inverse, (LOCAL, CELLS)), unroll=2)
    store.wait()


def write_kernel(raw_hbm, scale_ref, out_ref, buf, sem):
    loads = []
    for b in range(FB):
        x = pl.ds(16 * b, 16)
        loads.append(pltpu.make_async_copy(raw_hbm.at[x], buf.at[x], sem.at[FB * LOCAL + b]))
        loads[-1].start()
    stores = []
    scale = jnp.broadcast_to(scale_ref[:, 0:1], (LOCAL, PLANE))
    for b in range(FB):
        loads[b].wait()

        def body(c, scale):
            x = pl.ds(16 * b + 2 * c, 2)
            buf[x] = buf[x] * scale[None]
            return scale

        lax.fori_loop(0, 8, body, scale)
        x = pl.ds(16 * b, 16)
        for o in range(LOCAL):
            stores.append(pltpu.make_async_copy(buf.at[x, o, :], out_ref.at[o, x], sem.at[b * LOCAL + o]))
            stores[-1].start()
    for store in stores:
        store.wait()


VMEM_SPEC = pl.BlockSpec(memory_space=pltpu.VMEM)
SMEM_SPEC = pl.BlockSpec(memory_space=pltpu.SMEM)
HBM_SPEC = pl.BlockSpec(memory_space=pltpu.HBM)
PLANES = pltpu.VMEM((G + 4, LOCAL, PLANE), F32)
RAW = jax.ShapeDtypeStruct((G, LOCAL, PLANE), F32)
RAW_HBM = pltpu.HBM((G, LOCAL, PLANE), F32)
SCALE = jax.ShapeDtypeStruct((LOCAL, 128), F32)
SPREAD = jax.ShapeDtypeStruct((SLOTS, PIECE + 2, 128), F32)
HALVES = pltpu.VMEM((2 * TILES, G * LOCAL, 128), BF16)


def in_hbm(value):
    return pltpu.with_memory_space_constraint(value, pltpu.HBM)


def prepare_call(first, source, mats):
    return pl.pallas_call(
        functools.partial(prepare_kernel, first),
        out_shape=(RAW_HBM, RAW_HBM),
        in_specs=[HBM_SPEC] + [VMEM_SPEC] * len(source),
        out_specs=(HBM_SPEC, HBM_SPEC),
        scratch_shapes=[PLANES, pltpu.VMEM(RAW.shape, F32), HALVES]
        + [pltpu.SemaphoreType.DMA((FB * (LOCAL + 1) + STEPS,))],
        name="prepare_first" if first else "prepare_next",
        cost_estimate=pl.CostEstimate(flops=2 * 10**9, bytes_accessed=11 * 10**6, transcendentals=0),
        compiler_params=pltpu.CompilerParams(vmem_limit_bytes=BIG),
    )(in_hbm(source[0]), *source[1:], mats)


def filter_call(field, plain, mine, other, mats):
    return pl.pallas_call(
        filter_kernel,
        out_shape=(RAW_HBM, SCALE, SPREAD, SPREAD),
        in_specs=[HBM_SPEC] * 2 + [VMEM_SPEC] * 3,
        out_specs=(HBM_SPEC,) + (VMEM_SPEC,) * 3,
        scratch_shapes=[
            PLANES,
            PLANES,
            pltpu.VMEM(RAW.shape, F32),
            HALVES,
            HALVES,
            pltpu.VMEM((LOCAL, 128), F32),
            pltpu.SemaphoreType.DMA((2 * LOADS,)),
        ],
        name="filter",
        cost_estimate=pl.CostEstimate(flops=8 * 10**9, bytes_accessed=14 * 10**6, transcendentals=0),
        compiler_params=pltpu.CompilerParams(vmem_limit_bytes=BIG),
    )(in_hbm(field), in_hbm(plain), mine, other, mats)


def write_call(raw, scale):
    return pl.pallas_call(
        write_kernel,
        out_shape=pltpu.HBM((LOCAL, G, PLANE), F32),
        in_specs=[HBM_SPEC, VMEM_SPEC],
        out_specs=HBM_SPEC,
        scratch_shapes=[pltpu.VMEM(RAW.shape, F32), pltpu.SemaphoreType.DMA((FB * LOCAL + FB,))],
        name="write",
        cost_estimate=pl.CostEstimate(flops=10**6, bytes_accessed=11 * 10**6, transcendentals=0),
        compiler_params=pltpu.CompilerParams(vmem_limit_bytes=BIG),
    )(in_hbm(raw), scale)


def entry(blocks_ref, group, e):
    return blocks_ref[e % FB, 2 * group + e // FB]


def select_kernel(count, blocks_ref, *refs):
    group = lax.axis_index("frag")
    ins, outs, rows = refs[:4], refs[4:-1], refs[-1]
    for k in range(count):
        for s in range(N_FRAG):
            for e in range(ENT):
                for q in range(ROWS):
                    rows[k, s * ENT + e, pl.ds(q, 1), :] = ins[s][k, pl.ds(e, 1), pl.ds(128 * q, 128)]
    for k in range(count):
        for e in range(ENT):
            block = entry(blocks_ref, group, e)
            place = lax.rem(group - block // ENT + N_FRAG, N_FRAG) * ENT + lax.rem(block, ENT)
            outs[k][pl.ds(e * ROWS, ROWS), :] = rows[k, place]
            outs[count + k][pl.ds(e * ROWS, ROWS), :] = rows[k, e]


def select_call(blocks, arrays):
    count = arrays[0].shape[0]
    piece = jax.ShapeDtypeStruct((PIECE, 128), F32)
    out_shape = (piece,) * (2 * count)
    return pl.pallas_call(
        functools.partial(select_kernel, count),
        out_shape=out_shape,
        in_specs=[SMEM_SPEC] + [VMEM_SPEC] * 4,
        out_specs=(VMEM_SPEC,) * (2 * count),
        scratch_shapes=[pltpu.VMEM((count, N_FRAG * ENT, ROWS, 128), F32)],
        name=f"select{count}",
        compiler_params=pltpu.CompilerParams(vmem_limit_bytes=8 << 20),
    )(blocks, *arrays)


def place_kernel(blocks_hbm, p0_hbm, p1, p2, p3, out_ref, rows, p0, blocks_ref, sem):
    loads = [pltpu.make_async_copy(blocks_hbm, blocks_ref, sem.at[0]), pltpu.make_async_copy(p0_hbm, p0, sem.at[1])]
    for load in loads:
        load.start()
    group = lax.axis_index("frag")
    for s, ref in ((1, p1), (2, p2), (3, p3), (0, p0)):
        if s == 0:
            for load in loads:
                load.wait()
        for e in range(ENT):
            for q in range(ROWS):
                rows[s * ENT + e, pl.ds(q, 1), :] = ref[pl.ds(e, 1), pl.ds(128 * q, 128)]
    tail = jnp.zeros((2, 128), F32)
    for e in range(ENT):
        block = entry(blocks_ref, group, e)
        place = lax.rem(group - block // ENT + N_FRAG, N_FRAG) * ENT + lax.rem(block, ENT)
        value = rows[place]
        for slot in range(SLOTS):
            out_ref[slot, pl.ds(e * ROWS, ROWS), :] = value
    for slot in range(SLOTS):
        out_ref[slot, pl.ds(PIECE, 2), :] = tail


def place_call(blocks, pots):
    return pl.pallas_call(
        place_kernel,
        out_shape=SPREAD,
        in_specs=[HBM_SPEC] * 2 + [VMEM_SPEC] * 3,
        out_specs=VMEM_SPEC,
        scratch_shapes=[
            pltpu.VMEM((N_FRAG * ENT, ROWS, 128), F32),
            pltpu.VMEM((ENT, CELLS), F32),
            pltpu.SMEM((FB, 2 * N_FRAG), jnp.int32),
            pltpu.SemaphoreType.DMA((2,)),
        ],
        name="place",
        compiler_params=pltpu.CompilerParams(vmem_limit_bytes=8 << 20),
    )(in_hbm(blocks), in_hbm(pots[0]), *pots[1:])


def update_kernel(final, blocks_ref, signs_ref, core_ref, ion_ref, d0, d1, d2, d3, out_ref):
    group = lax.axis_index("frag")
    seen = []
    for s, d in enumerate((d0, d1, d2, d3)):
        source = lax.rem(group - s + N_FRAG, N_FRAG)
        for k in range(ENT):
            sign = jnp.where(signs_ref[2 * source + k // FB] > 0, 1.0 / ORBS, -1.0 / ORBS)
            seen.append((entry(blocks_ref, source, k), sign.astype(F32), d[pl.ds(k * ROWS, ROWS), :]))
    for e in range(ENT):
        mine = group * ENT + e if final else entry(blocks_ref, group, e)
        total = core_ref[pl.ds(e * ROWS, ROWS), :]
        for block, sign, density in seen:
            total = total + jnp.where(block == mine, sign, jnp.float32(0.0)) * density
        total = jnp.maximum(total, DENSITY_FLOOR)
        root = jnp.exp(jnp.log(total) * (1.0 / 3.0))
        root = root - (root * root * root - total) / (3.0 * root * root)
        value = ion_ref[pl.ds(e * ROWS, ROWS), :] - EXCHANGE_COEF * root
        if final:
            for q in range(ROWS):
                out_ref[pl.ds(e, 1), pl.ds(128 * q, 128)] = value[q : q + 1]
        else:
            for slot in range(SLOTS):
                out_ref[slot, pl.ds(e * ROWS, ROWS), :] = value
    if not final:
        for slot in range(SLOTS):
            out_ref[slot, pl.ds(PIECE, 2), :] = jnp.zeros((2, 128), F32)


def update_call(final, blocks, signs, core, ion, densities):
    return pl.pallas_call(
        functools.partial(update_kernel, final),
        out_shape=jax.ShapeDtypeStruct((ENT, CELLS), F32) if final else SPREAD,
        in_specs=[SMEM_SPEC] * 2 + [VMEM_SPEC] * 6,
        out_specs=VMEM_SPEC,
        name="update_last" if final else "update_first",
        compiler_params=pltpu.CompilerParams(vmem_limit_bytes=8 << 20),
    )(blocks, signs, core, ion, *densities)


def frag_all(value):
    return [value] + [
        lax.ppermute(value, "frag", [(g, (g + s) % N_FRAG) for g in range(N_FRAG)]) for s in (1, 2, 3)
    ]


def core_swap(value):
    return lax.ppermute(value, "orb", [(i, i ^ 1) for i in range(2 * SLOTS)])


def plane_exchange(value):
    groups = [[2 * i + c for i in range(SLOTS)] for c in range(2)]
    return lax.all_to_all(value, "orb", 0, 0, axis_index_groups=groups, tiled=True)


def shards(orbitals, potential, ion_potential, core_density, frag_blocks, frag_signs):
    blocks = frag_blocks.T
    mats = stencil_matrices().reshape(3, WIN, 2, 128).transpose(0, 2, 1, 3)
    mats = jnp.asarray(mats, BF16)

    pots = frag_all(potential)
    spread, source = lax.optimization_barrier((place_call(blocks, pots), orbitals.reshape(LOCAL, G, PLANE)))
    near = plane_exchange(spread)
    field, plain = prepare_call(True, (source,), mats)
    near, field = lax.optimization_barrier((near, field))
    statics = frag_all(jnp.stack([core_density, ion_potential]))
    raw, scale, mine, other = filter_call(field, plain, near, core_swap(near), mats)
    cores, ions, own_core, own_ion = select_call(blocks, statics)

    density = plane_exchange(mine + core_swap(other))
    densities = frag_all(jnp.sum(density, axis=0))
    spread = update_call(False, blocks, frag_signs, cores, ions, densities)
    spread, raw = lax.optimization_barrier((spread, raw))
    near = plane_exchange(spread)
    field, plain = prepare_call(False, (raw, scale), mats)
    near, field = lax.optimization_barrier((near, field))
    raw, scale, mine, other = filter_call(field, plain, near, core_swap(near), mats)

    density, raw = lax.optimization_barrier((mine + core_swap(other), raw))
    density = plane_exchange(density)
    filtered = write_call(raw, scale)
    density, filtered = lax.optimization_barrier((density, filtered))
    densities = frag_all(jnp.sum(density, axis=0))
    new_potential = update_call(True, blocks, frag_signs, own_core, own_ion, densities)
    return (filtered.reshape(orbitals.shape), new_potential)


def solution(mesh):
    in_specs = (
        P("frag", "orb", None, None),
        P("frag", "orb"),
        P("frag", "orb"),
        P("frag", "orb"),
        P(),
        P(),
    )
    out_specs = (P("frag", "orb", None, None), P("frag", "orb"))
    return jax.shard_map(shards, mesh=mesh, in_specs=in_specs, out_specs=out_specs, check_vma=False)
```

```python
import functools

import jax
import jax.numpy as jnp
import numpy as np
from jax import lax
from jax.experimental import pallas as pl
from jax.experimental.pallas import tpu as pltpu
from jax.sharding import PartitionSpec as P

G = 48
PLANE = G * G
FB = 3
ORBS = 128
N_FRAG = 4
SLOTS = 16
BAND = 64
BANDS = 6
UNROLL = 4
LOADS = 6
XLOAD = G // LOADS
BIG = 40 << 20
ENT = 6
CELLS = 1152
ROWS = CELLS // 128
PIECE = ENT * ROWS
LOCAL = 8
COLS = 256
WIN = 512
STEPS = PLANE // COLS
TILES = PLANE // 128 + 2
DENSITY_FLOOR = 0.25
EXCHANGE_COEF = 0.9847450218426965
NORM_EPS = 1e-6
F32 = jnp.float32
BF16 = jnp.bfloat16


def stencil_matrices():
    mats = np.zeros((3, WIN, COLS), np.float32)
    for phase in range(3):
        out = 768 + COLS * phase + np.arange(COLS)[None, :]
        src = 768 + COLS * phase - 128 + np.arange(WIN)[:, None]
        diff = np.abs(src - out)
        same = (src // G) == (out // G)
        mats[phase] = (
            np.where(diff == G, -16.0, 0.0)
            + np.where(diff == 2 * G, 1.0, 0.0)
            + np.where((diff == 1) & same, -16.0, 0.0)
            + np.where((diff == 2) & same, 1.0, 0.0)
        )
    return mats


def split(values):
    high = values.astype(BF16)
    low = (values - high.astype(F32)).astype(BF16)
    return high, low


def cols(start, size=128):
    return pl.ds(pl.multiple_of(start, 128), size)


def zero_planes(buf):
    buf[pl.ds(0, 2)] = jnp.zeros((2, LOCAL, PLANE), F32)
    buf[pl.ds(G + 2, 2)] = jnp.zeros((2, LOCAL, PLANE), F32)


def zero_margins(halves):
    for part in range(2):
        halves[part * TILES] = jnp.zeros((G * LOCAL, 128), BF16)
        halves[part * TILES + TILES - 1] = jnp.zeros((G * LOCAL, 128), BF16)


def put_halves(halves, c, values):
    rows = pl.ds(pl.multiple_of(16 * c, 16), 16)
    for j in range(TILES - 2):
        high, low = split(values[:, :, 128 * j : 128 * j + 128].reshape(16, 128))
        halves[1 + j, rows, :] = high
        halves[TILES + 1 + j, rows, :] = low


def run_chain(apps, mats_ref):
    def scoped(*accs):
        def acc(parity, unit, i):
            return accs[(2 * parity + unit) * BANDS + i]

        def push(n, parity, unit):
            mat = jnp.concatenate([mats_ref[lax.rem(n, 3), t, pl.ds(COLS * unit, COLS), :] for t in range(2)], axis=1)
            pltpu.matmul_push_rhs(mat, staging_register=parity, mxu_index=unit)

        def feed(app, n, parity, i):
            halves = app[5]
            rows = pl.ds(BAND * i, BAND)
            for unit in range(2):
                high, low = (
                    jnp.concatenate([halves[part * TILES + 2 * (n + unit) + t, rows, :] for t in range(2)], axis=1)
                    for part in range(2)
                )
                pltpu.matmul_acc_lhs(acc(parity, unit, i), high, load_staged_rhs=parity if i == 0 else None)
                pltpu.matmul_acc_lhs(acc(parity, unit, i), low)
                if i == BANDS - 2 + unit:
                    push(n + 1, 1 - parity, unit)

        def emit(app, n, parity, i):
            kind, cur, prev, dst, wf, _, halves_next, sums, done = app
            rows = pl.ds(BAND * i, BAND)
            values = pltpu.matmul_pop(acc(parity, 0, i)) + pltpu.matmul_pop(acc(parity, 1, i))
            for t in range(COLS // 128):
                lane = cols(COLS * n + 128 * t)
                near = cur[pl.ds(8 * i, 12), :, lane]
                s1 = near[1:9] + near[3:11]
                s2 = near[0:8] + near[4:12]
                plane = values[:, 128 * t : 128 * t + 128].reshape(8, LOCAL, 128)
                new = plane + s2 - 16.0 * s1
                here = pl.ds(8 * i + (0 if kind == "plain" else 2), 8)
                if kind == "plain":
                    dst[here, :, lane] = (0.5 / 48.0) * new
                    continue
                new = (1.0 / 48.0) * new + wf[pl.ds(8 * i, 8), :, lane] * near[2:10]
                new = new - prev[pl.ds(8 * i + 2, 8), :, lane]
                dst[here, :, lane] = new
                if kind == "last":
                    sums[...] += jnp.sum(new * new, axis=0)
                else:
                    high, low = split(new.reshape(BAND, 128))
                    halves_next[2 * n + t + 1, rows, :] = high
                    halves_next[TILES + 2 * n + t + 1, rows, :] = low
            if done is not None and i == BANDS - 1:
                done(n)

        for unit in range(2):
            push(0, 0, unit)
        for i in range(BANDS):
            feed(apps[0], 0, 0, i)
        for number, app in enumerate(apps):

            def body(j, carry):
                for u in range(UNROLL):
                    for i in range(BANDS):
                        feed(app, UNROLL * j + u + 1, (number + u + 1) % 2, i)
                        emit(app, UNROLL * j + u, (number + u) % 2, i)
                return carry

            lax.fori_loop(0, STEPS // UNROLL, body, 0)
            for i in range(BANDS):
                if number + 1 < len(apps):
                    feed(apps[number + 1], 0, (number + 1) % 2, i)
                emit(app, STEPS - 1, number % 2, i)
        rest = len(apps) % 2
        for unit in range(2):
            pltpu.matmul_acc_lhs(acc(rest, unit, 0), jnp.zeros((BAND, COLS), BF16), load_staged_rhs=rest)
            pltpu.matmul_pop(acc(rest, unit, 0))

    pl.run_scoped(
        scoped,
        *[pltpu.ACC(unit)((BAND, COLS), F32) for _ in range(2) for unit in range(2) for _ in range(BANDS)],
    )


def prepare_kernel(first, source, *refs):
    if first:
        mats_ref, field_hbm, plain_hbm, field, plain, hl, sem = refs
    else:
        scale_ref, mats_ref, field_hbm, plain_hbm, field, plain, hl, sem = refs
    loads = []
    for p in range(FB):
        inner = pl.ds(2 + 16 * p, 16)
        x = pl.ds(16 * p, 16)
        if first:
            loads.append(
                [
                    pltpu.make_async_copy(source.at[o, x], field.at[inner, o, :], sem.at[LOCAL * p + o])
                    for o in range(LOCAL)
                ]
            )
        else:
            loads.append([pltpu.make_async_copy(source.at[x], field.at[inner], sem.at[LOCAL * p])])
        for load in loads[-1]:
            load.start()
    zero_planes(field)
    zero_margins(hl)
    scale = None if first else jnp.broadcast_to(scale_ref[:, 0:1], (LOCAL, PLANE))

    def body(c, scale):
        x = pl.ds(2 + 2 * c, 2)
        values = field[x]
        if not first:
            values = values * scale[None]
            field[x] = values
        put_halves(hl, c, values)
        return scale

    stores = []
    for p in range(FB):
        for load in loads[p]:
            load.wait()
        lax.fori_loop(8 * p, 8 * p + 8, body, scale)
        stores.append(
            pltpu.make_async_copy(
                field.at[pl.ds(2 + 16 * p, 16)], field_hbm.at[pl.ds(16 * p, 16)], sem.at[FB * LOCAL + p]
            )
        )
        stores[-1].start()

    def column(n):
        lane = cols(COLS * n, COLS)
        return pltpu.make_async_copy(plain.at[:, :, lane], plain_hbm.at[:, :, lane], sem.at[FB * (LOCAL + 1) + n])

    run_chain([("plain", field, None, plain, None, hl, None, None, lambda n: column(n).start())], mats_ref)
    for store in stores:
        store.wait()
    for n in range(STEPS):
        column(n).wait()


def filter_kernel(final, field_hbm, plain_hbm, mine_ref, other_ref, mats_ref, out_hbm, scale_ref, dmine_ref,
                  dother_ref, ya, yb, wf, hl0, hl1, sums, sem):
    core = lax.axis_index("orb") % 2
    loads = []
    for p in range(LOADS):
        x = pl.ds(XLOAD * p, XLOAD)
        inner = pl.ds(2 + XLOAD * p, XLOAD)
        loads.append(pltpu.make_async_copy(field_hbm.at[x], ya.at[inner], sem.at[2 * p]))
        loads.append(pltpu.make_async_copy(plain_hbm.at[x], yb.at[inner], sem.at[2 * p + 1]))
    for load in loads:
        load.start()
    upper = lax.broadcasted_iota(jnp.int32, (LOCAL, 128), 0) >= LOCAL // 2

    def build(row, carry):
        for ref, half in ((mine_ref, core), (other_ref, 1 - core)):
            for b in range(FB):
                tiles = []
                for q in range(ROWS):
                    v0 = ref[row, pl.ds(b * ROWS + q, 1), :]
                    v1 = ref[row, pl.ds((FB + b) * ROWS + q, 1), :]
                    v = jnp.where(upper, jnp.broadcast_to(v1, (LOCAL, 128)), jnp.broadcast_to(v0, (LOCAL, 128)))
                    tiles.append(v * 0.125 - 0.375)
                wf[16 * b + row, :, cols(half * CELLS, CELLS)] = jnp.concatenate(tiles, axis=1)
        return carry

    lax.fori_loop(0, SLOTS, build, 0, unroll=2)
    zero_planes(ya)
    zero_planes(yb)
    zero_margins(hl0)
    zero_margins(hl1)
    sums[...] = jnp.zeros((LOCAL, 128), F32)

    def start(c, carry):
        x = pl.ds(2 + 2 * c, 2)
        value = yb[x] + 0.5 * (wf[pl.ds(2 * c, 2)] * ya[x])
        yb[x] = value
        put_halves(hl0, c, value)
        return carry

    for p in range(LOADS):
        loads[2 * p].wait()
        loads[2 * p + 1].wait()
        lax.fori_loop(p * XLOAD // 2, (p + 1) * XLOAD // 2, start, 0)
    run_chain(
        [
            ("middle", yb, ya, ya, wf, hl0, hl1, sums, None),
            ("middle", ya, yb, yb, wf, hl1, hl0, sums, None),
            ("last", yb, ya, ya, wf, hl0, None, sums, None),
        ],
        mats_ref,
    )
    stores = []
    if not final:
        stores.append(pltpu.make_async_copy(ya.at[pl.ds(2, G)], out_hbm, sem.at[0]))
        stores[-1].start()
    mean = jnp.sum(sums[...], axis=1, keepdims=True) * (1.0 / (G * PLANE))
    inverse = 1.0 / jnp.sqrt(mean + NORM_EPS)
    scale_ref[...] = jnp.broadcast_to(inverse, (LOCAL, 128))

    def finish(b, row, scale):
        for ref, half in ((dmine_ref, core), (dother_ref, 1 - core)):
            lane = cols(half * CELLS, CELLS)
            value = ya[2 + 16 * b + row, :, lane] * scale
            if final:
                yb[2 + 16 * b + row, :, lane] = value
            value = value * value
            value = value + pltpu.roll(value, 1, 0)
            value = value + pltpu.roll(value, 2, 0)
            for q in range(ROWS):
                ref[SLOTS - 1 - row, pl.ds(b * ROWS + q, 1), :] = value[3:4, 128 * q : 128 * q + 128]
                ref[SLOTS - 1 - row, pl.ds((FB + b) * ROWS + q, 1), :] = value[7:8, 128 * q : 128 * q + 128]
            if b == 0:
                ref[SLOTS - 1 - row, pl.ds(PIECE, 2), :] = jnp.zeros((2, 128), F32)
        return scale

    scale = jnp.broadcast_to(inverse, (LOCAL, CELLS))
    for b in range(FB):
        scale = lax.fori_loop(0, SLOTS, functools.partial(finish, b), scale, unroll=4)
        if final:
            for o in range(LOCAL):
                stores.append(
                    pltpu.make_async_copy(
                        yb.at[pl.ds(2 + 16 * b, 16), o, :], out_hbm.at[o, pl.ds(16 * b, 16)], sem.at[b * LOCAL + o]
                    )
                )
                stores[-1].start()
    for store in stores:
        store.wait()


VMEM_SPEC = pl.BlockSpec(memory_space=pltpu.VMEM)
SMEM_SPEC = pl.BlockSpec(memory_space=pltpu.SMEM)
HBM_SPEC = pl.BlockSpec(memory_space=pltpu.HBM)
PLANES = pltpu.VMEM((G + 4, LOCAL, PLANE), F32)
RAW = jax.ShapeDtypeStruct((G, LOCAL, PLANE), F32)
RAW_HBM = pltpu.HBM((G, LOCAL, PLANE), F32)
SCALE = jax.ShapeDtypeStruct((LOCAL, 128), F32)
SPREAD = jax.ShapeDtypeStruct((SLOTS, PIECE + 2, 128), F32)
HALVES = pltpu.VMEM((2 * TILES, G * LOCAL, 128), BF16)


def in_hbm(value):
    return pltpu.with_memory_space_constraint(value, pltpu.HBM)


def prepare_call(first, source, mats):
    return pl.pallas_call(
        functools.partial(prepare_kernel, first),
        out_shape=(RAW_HBM, RAW_HBM),
        in_specs=[HBM_SPEC] + [VMEM_SPEC] * len(source),
        out_specs=(HBM_SPEC, HBM_SPEC),
        scratch_shapes=[PLANES, pltpu.VMEM(RAW.shape, F32), HALVES]
        + [pltpu.SemaphoreType.DMA((FB * (LOCAL + 1) + STEPS,))],
        name="prepare_first" if first else "prepare_next",
        cost_estimate=pl.CostEstimate(flops=2 * 10**9, bytes_accessed=11 * 10**6, transcendentals=0),
        compiler_params=pltpu.CompilerParams(vmem_limit_bytes=BIG),
    )(in_hbm(source[0]), *source[1:], mats)


def filter_call(final, field, plain, mine, other, mats):
    return pl.pallas_call(
        functools.partial(filter_kernel, final),
        out_shape=(pltpu.HBM((LOCAL, G, PLANE), F32) if final else RAW_HBM, SCALE, SPREAD, SPREAD),
        in_specs=[HBM_SPEC] * 2 + [VMEM_SPEC] * 3,
        out_specs=(HBM_SPEC,) + (VMEM_SPEC,) * 3,
        scratch_shapes=[
            PLANES,
            PLANES,
            pltpu.VMEM(RAW.shape, F32),
            HALVES,
            HALVES,
            pltpu.VMEM((LOCAL, 128), F32),
            pltpu.SemaphoreType.DMA((FB * LOCAL,)),
        ],
        name="filter_last" if final else "filter_first",
        cost_estimate=pl.CostEstimate(flops=8 * 10**9, bytes_accessed=14 * 10**6, transcendentals=0),
        compiler_params=pltpu.CompilerParams(vmem_limit_bytes=BIG),
    )(in_hbm(field), in_hbm(plain), mine, other, mats)


def entry(blocks_ref, group, e):
    return blocks_ref[e % FB, 2 * group + e // FB]


def select_kernel(count, blocks_ref, *refs):
    group = lax.axis_index("frag")
    ins, outs, rows = refs[:4], refs[4:-1], refs[-1]
    for k in range(count):
        for s in range(N_FRAG):
            for e in range(ENT):
                for q in range(ROWS):
                    rows[k, s * ENT + e, pl.ds(q, 1), :] = ins[s][k, pl.ds(e, 1), pl.ds(128 * q, 128)]
    for k in range(count):
        for e in range(ENT):
            block = entry(blocks_ref, group, e)
            place = lax.rem(group - block // ENT + N_FRAG, N_FRAG) * ENT + lax.rem(block, ENT)
            outs[k][pl.ds(e * ROWS, ROWS), :] = rows[k, place]
            outs[count + k][pl.ds(e * ROWS, ROWS), :] = rows[k, e]


def select_call(blocks, arrays):
    count = arrays[0].shape[0]
    piece = jax.ShapeDtypeStruct((PIECE, 128), F32)
    out_shape = (piece,) * (2 * count)
    return pl.pallas_call(
        functools.partial(select_kernel, count),
        out_shape=out_shape,
        in_specs=[SMEM_SPEC] + [VMEM_SPEC] * 4,
        out_specs=(VMEM_SPEC,) * (2 * count),
        scratch_shapes=[pltpu.VMEM((count, N_FRAG * ENT, ROWS, 128), F32)],
        name=f"select{count}",
        compiler_params=pltpu.CompilerParams(vmem_limit_bytes=8 << 20),
    )(blocks, *arrays)


def place_kernel(blocks_hbm, p0_hbm, p1, p2, p3, out_ref, rows, p0, blocks_ref, sem):
    loads = [pltpu.make_async_copy(blocks_hbm, blocks_ref, sem.at[0]), pltpu.make_async_copy(p0_hbm, p0, sem.at[1])]
    for load in loads:
        load.start()
    group = lax.axis_index("frag")
    for s, ref in ((1, p1), (2, p2), (3, p3), (0, p0)):
        if s == 0:
            for load in loads:
                load.wait()
        for e in range(ENT):
            for q in range(ROWS):
                rows[s * ENT + e, pl.ds(q, 1), :] = ref[pl.ds(e, 1), pl.ds(128 * q, 128)]
    tail = jnp.zeros((2, 128), F32)
    for e in range(ENT):
        block = entry(blocks_ref, group, e)
        place = lax.rem(group - block // ENT + N_FRAG, N_FRAG) * ENT + lax.rem(block, ENT)
        value = rows[place]
        for slot in range(SLOTS):
            out_ref[slot, pl.ds(e * ROWS, ROWS), :] = value
    for slot in range(SLOTS):
        out_ref[slot, pl.ds(PIECE, 2), :] = tail


def place_call(blocks, pots):
    return pl.pallas_call(
        place_kernel,
        out_shape=SPREAD,
        in_specs=[HBM_SPEC] * 2 + [VMEM_SPEC] * 3,
        out_specs=VMEM_SPEC,
        scratch_shapes=[
            pltpu.VMEM((N_FRAG * ENT, ROWS, 128), F32),
            pltpu.VMEM((ENT, CELLS), F32),
            pltpu.SMEM((FB, 2 * N_FRAG), jnp.int32),
            pltpu.SemaphoreType.DMA((2,)),
        ],
        name="place",
        compiler_params=pltpu.CompilerParams(vmem_limit_bytes=8 << 20),
    )(in_hbm(blocks), in_hbm(pots[0]), *pots[1:])


def update_kernel(final, blocks_ref, signs_ref, core_ref, ion_ref, d0, d1, d2, d3, out_ref):
    group = lax.axis_index("frag")
    seen = []
    for s, d in enumerate((d0, d1, d2, d3)):
        source = lax.rem(group - s + N_FRAG, N_FRAG)
        for k in range(ENT):
            sign = jnp.where(signs_ref[2 * source + k // FB] > 0, 1.0 / ORBS, -1.0 / ORBS)
            seen.append((entry(blocks_ref, source, k), sign.astype(F32), d[pl.ds(k * ROWS, ROWS), :]))
    for e in range(ENT):
        mine = group * ENT + e if final else entry(blocks_ref, group, e)
        total = core_ref[pl.ds(e * ROWS, ROWS), :]
        for block, sign, density in seen:
            total = total + jnp.where(block == mine, sign, jnp.float32(0.0)) * density
        total = jnp.maximum(total, DENSITY_FLOOR)
        root = jnp.exp(jnp.log(total) * (1.0 / 3.0))
        root = root - (root * root * root - total) / (3.0 * root * root)
        value = ion_ref[pl.ds(e * ROWS, ROWS), :] - EXCHANGE_COEF * root
        if final:
            for q in range(ROWS):
                out_ref[pl.ds(e, 1), pl.ds(128 * q, 128)] = value[q : q + 1]
        else:
            for slot in range(SLOTS):
                out_ref[slot, pl.ds(e * ROWS, ROWS), :] = value
    if not final:
        for slot in range(SLOTS):
            out_ref[slot, pl.ds(PIECE, 2), :] = jnp.zeros((2, 128), F32)


def update_call(final, blocks, signs, core, ion, densities):
    return pl.pallas_call(
        functools.partial(update_kernel, final),
        out_shape=jax.ShapeDtypeStruct((ENT, CELLS), F32) if final else SPREAD,
        in_specs=[SMEM_SPEC] * 2 + [VMEM_SPEC] * 6,
        out_specs=VMEM_SPEC,
        name="update_last" if final else "update_first",
        compiler_params=pltpu.CompilerParams(vmem_limit_bytes=8 << 20),
    )(blocks, signs, core, ion, *densities)


def frag_all(value):
    return [value] + [
        lax.ppermute(value, "frag", [(g, (g + s) % N_FRAG) for g in range(N_FRAG)]) for s in (1, 2, 3)
    ]


def core_swap(value):
    return lax.ppermute(value, "orb", [(i, i ^ 1) for i in range(2 * SLOTS)])


def plane_exchange(value, backward=False):
    order = range(SLOTS - 1, -1, -1) if backward else range(SLOTS)
    groups = [[2 * i + c for i in order] for c in range(2)]
    return lax.all_to_all(value, "orb", 0, 0, axis_index_groups=groups, tiled=True)


def shards(orbitals, potential, ion_potential, core_density, frag_blocks, frag_signs):
    blocks = frag_blocks.T
    mats = stencil_matrices().reshape(3, WIN, 2, 128).transpose(0, 2, 1, 3)
    mats = jnp.asarray(mats, BF16)

    pots = frag_all(potential)
    spread, source = lax.optimization_barrier((place_call(blocks, pots), orbitals.reshape(LOCAL, G, PLANE)))
    near = plane_exchange(spread)
    field, plain = prepare_call(True, (source,), mats)
    near, field = lax.optimization_barrier((near, field))
    statics = frag_all(jnp.stack([core_density, ion_potential]))
    raw, scale, mine, other = filter_call(False, field, plain, near, core_swap(near), mats)
    cores, ions, own_core, own_ion = select_call(blocks, statics)

    density = plane_exchange(mine + core_swap(other), backward=True)
    densities = frag_all(jnp.sum(density, axis=0))
    spread = update_call(False, blocks, frag_signs, cores, ions, densities)
    spread, raw = lax.optimization_barrier((spread, raw))
    near = plane_exchange(spread)
    field, plain = prepare_call(False, (raw, scale), mats)
    near, field = lax.optimization_barrier((near, field))
    filtered, _, mine, other = filter_call(True, field, plain, near, core_swap(near), mats)
    density = plane_exchange(mine + core_swap(other), backward=True)
    densities = frag_all(jnp.sum(density, axis=0))
    new_potential = update_call(True, blocks, frag_signs, own_core, own_ion, densities)
    return (filtered.reshape(orbitals.shape), new_potential)


def solution(mesh):
    in_specs = (
        P("frag", "orb", None, None),
        P("frag", "orb"),
        P("frag", "orb"),
        P("frag", "orb"),
        P(),
        P(),
    )
    out_specs = (P("frag", "orb", None, None), P("frag", "orb"))
    return jax.shard_map(shards, mesh=mesh, in_specs=in_specs, out_specs=out_specs, check_vma=False)
```

```python
import functools

import jax
import jax.numpy as jnp
import numpy as np
from jax import lax
from jax.experimental import pallas as pl
from jax.experimental.pallas import tpu as pltpu
from jax.sharding import PartitionSpec as P

G = 48
PLANE = G * G
FB = 3
ORBS = 128
N_FRAG = 4
SLOTS = 16
BAND = 64
BANDS = 6
UNROLL = 4
LOADS = 6
XLOAD = G // LOADS
BIG = 40 << 20
ENT = 6
CELLS = 1152
ROWS = CELLS // 128
PIECE = ENT * ROWS
LOCAL = 8
COLS = 256
WIN = 512
STEPS = PLANE // COLS
TILES = PLANE // 128 + 2
DENSITY_FLOOR = 0.25
EXCHANGE_COEF = 0.9847450218426965
NORM_EPS = 1e-6
F32 = jnp.float32
BF16 = jnp.bfloat16


def stencil_matrices():
    mats = np.zeros((3, WIN, COLS), np.float32)
    for phase in range(3):
        out = 768 + COLS * phase + np.arange(COLS)[None, :]
        src = 768 + COLS * phase - 128 + np.arange(WIN)[:, None]
        diff = np.abs(src - out)
        same = (src // G) == (out // G)
        mats[phase] = (
            np.where(diff == G, -16.0, 0.0)
            + np.where(diff == 2 * G, 1.0, 0.0)
            + np.where((diff == 1) & same, -16.0, 0.0)
            + np.where((diff == 2) & same, 1.0, 0.0)
        )
    return mats


def split(values):
    high = values.astype(BF16)
    low = (values - high.astype(F32)).astype(BF16)
    return high, low


def cols(start, size=128):
    return pl.ds(pl.multiple_of(start, 128), size)


def zero_planes(buf):
    buf[pl.ds(0, 2)] = jnp.zeros((2, LOCAL, PLANE), F32)
    buf[pl.ds(G + 2, 2)] = jnp.zeros((2, LOCAL, PLANE), F32)


def zero_margins(halves):
    for part in range(2):
        halves[part * TILES] = jnp.zeros((G * LOCAL, 128), BF16)
        halves[part * TILES + TILES - 1] = jnp.zeros((G * LOCAL, 128), BF16)


def put_halves(halves, c, values):
    rows = pl.ds(pl.multiple_of(16 * c, 16), 16)
    for j in range(TILES - 2):
        high, low = split(values[:, :, 128 * j : 128 * j + 128].reshape(16, 128))
        halves[1 + j, rows, :] = high
        halves[TILES + 1 + j, rows, :] = low


def run_chain(apps, mats_ref):
    def scoped(*accs):
        def acc(parity, unit, i):
            return accs[(2 * parity + unit) * BANDS + i]

        def push(n, parity, unit):
            mat = jnp.concatenate([mats_ref[lax.rem(n, 3), t, pl.ds(COLS * unit, COLS), :] for t in range(2)], axis=1)
            pltpu.matmul_push_rhs(mat, staging_register=parity, mxu_index=unit)

        def feed(app, n, parity, i):
            halves = app[5]
            rows = pl.ds(BAND * i, BAND)
            for unit in range(2):
                high, low = (
                    jnp.concatenate([halves[part * TILES + 2 * (n + unit) + t, rows, :] for t in range(2)], axis=1)
                    for part in range(2)
                )
                pltpu.matmul_acc_lhs(acc(parity, unit, i), high, load_staged_rhs=parity if i == 0 else None)
                pltpu.matmul_acc_lhs(acc(parity, unit, i), low)
                if i == BANDS - 2 + unit:
                    push(n + 1, 1 - parity, unit)

        def emit(app, n, parity, i):
            kind, cur, prev, dst, wf, _, halves_next, sums, done = app
            rows = pl.ds(BAND * i, BAND)
            values = pltpu.matmul_pop(acc(parity, 0, i)) + pltpu.matmul_pop(acc(parity, 1, i))
            for t in range(COLS // 128):
                lane = cols(COLS * n + 128 * t)
                near = cur[pl.ds(8 * i, 12), :, lane]
                s1 = near[1:9] + near[3:11]
                s2 = near[0:8] + near[4:12]
                plane = values[:, 128 * t : 128 * t + 128].reshape(8, LOCAL, 128)
                new = plane + s2 - 16.0 * s1
                here = pl.ds(8 * i + (0 if kind == "plain" else 2), 8)
                if kind == "plain":
                    dst[here, :, lane] = (0.5 / 48.0) * new
                    continue
                new = (1.0 / 48.0) * new + wf[pl.ds(8 * i, 8), :, lane] * near[2:10]
                new = new - prev[pl.ds(8 * i + 2, 8), :, lane]
                dst[here, :, lane] = new
                if kind == "last":
                    sums[...] += jnp.sum(new * new, axis=0)
                else:
                    high, low = split(new.reshape(BAND, 128))
                    halves_next[2 * n + t + 1, rows, :] = high
                    halves_next[TILES + 2 * n + t + 1, rows, :] = low
            if done is not None and i == BANDS - 1:
                done(n)

        for unit in range(2):
            push(0, 0, unit)
        for i in range(BANDS):
            feed(apps[0], 0, 0, i)
        for number, app in enumerate(apps):

            def body(j, carry):
                for u in range(UNROLL):
                    for i in range(BANDS):
                        feed(app, UNROLL * j + u + 1, (number + u + 1) % 2, i)
                        emit(app, UNROLL * j + u, (number + u) % 2, i)
                return carry

            lax.fori_loop(0, STEPS // UNROLL, body, 0)
            for i in range(BANDS):
                if number + 1 < len(apps):
                    feed(apps[number + 1], 0, (number + 1) % 2, i)
                emit(app, STEPS - 1, number % 2, i)
        rest = len(apps) % 2
        for unit in range(2):
            pltpu.matmul_acc_lhs(acc(rest, unit, 0), jnp.zeros((BAND, COLS), BF16), load_staged_rhs=rest)
            pltpu.matmul_pop(acc(rest, unit, 0))

    pl.run_scoped(
        scoped,
        *[pltpu.ACC(unit)((BAND, COLS), F32) for _ in range(2) for unit in range(2) for _ in range(BANDS)],
    )


def prepare_kernel(first, source, *refs):
    if first:
        mats_ref, field_hbm, plain_hbm, field, plain, hl, sem = refs
    else:
        scale_ref, mats_ref, field_hbm, plain_hbm, field, plain, hl, sem = refs
    loads = []
    for p in range(FB):
        inner = pl.ds(2 + 16 * p, 16)
        x = pl.ds(16 * p, 16)
        if first:
            loads.append(
                [
                    pltpu.make_async_copy(source.at[o, x], field.at[inner, o, :], sem.at[LOCAL * p + o])
                    for o in range(LOCAL)
                ]
            )
        else:
            loads.append([pltpu.make_async_copy(source.at[x], field.at[inner], sem.at[LOCAL * p])])
        for load in loads[-1]:
            load.start()
    zero_planes(field)
    zero_margins(hl)
    scale = None if first else jnp.broadcast_to(scale_ref[:, 0:1], (LOCAL, PLANE))

    def body(c, scale):
        x = pl.ds(2 + 2 * c, 2)
        values = field[x]
        if not first:
            values = values * scale[None]
            field[x] = values
        put_halves(hl, c, values)
        return scale

    stores = []
    for p in range(FB):
        for load in loads[p]:
            load.wait()
        lax.fori_loop(8 * p, 8 * p + 8, body, scale)
        stores.append(
            pltpu.make_async_copy(
                field.at[pl.ds(2 + 16 * p, 16)], field_hbm.at[pl.ds(16 * p, 16)], sem.at[FB * LOCAL + p]
            )
        )
        stores[-1].start()

    def column(n):
        lane = cols(COLS * n, COLS)
        return pltpu.make_async_copy(plain.at[:, :, lane], plain_hbm.at[:, :, lane], sem.at[FB * (LOCAL + 1) + n])

    run_chain([("plain", field, None, plain, None, hl, None, None, lambda n: column(n).start())], mats_ref)
    for store in stores:
        store.wait()
    for n in range(STEPS):
        column(n).wait()


def filter_kernel(final, field_hbm, plain_hbm, mine_ref, other_ref, mats_ref, out_hbm, scale_ref, dmine_ref,
                  dother_ref, ya, yb, wf, hl0, hl1, sums, sem):
    core = lax.axis_index("orb") % 2
    loads = []
    for p in range(LOADS):
        x = pl.ds(XLOAD * p, XLOAD)
        inner = pl.ds(2 + XLOAD * p, XLOAD)
        loads.append(pltpu.make_async_copy(field_hbm.at[x], ya.at[inner], sem.at[2 * p]))
        loads.append(pltpu.make_async_copy(plain_hbm.at[x], yb.at[inner], sem.at[2 * p + 1]))
    for load in loads:
        load.start()
    upper = lax.broadcasted_iota(jnp.int32, (LOCAL, 128), 0) >= LOCAL // 2

    def build(row, carry):
        slot = SLOTS - 1 - row if final else row
        for ref, half in ((mine_ref, core), (other_ref, 1 - core)):
            for b in range(FB):
                tiles = []
                for q in range(ROWS):
                    v0 = ref[slot, pl.ds(b * ROWS + q, 1), :]
                    v1 = ref[slot, pl.ds((FB + b) * ROWS + q, 1), :]
                    v = jnp.where(upper, jnp.broadcast_to(v1, (LOCAL, 128)), jnp.broadcast_to(v0, (LOCAL, 128)))
                    tiles.append(v * 0.125 - 0.375)
                wf[16 * b + row, :, cols(half * CELLS, CELLS)] = jnp.concatenate(tiles, axis=1)
        return carry

    lax.fori_loop(0, SLOTS, build, 0, unroll=2)
    zero_planes(ya)
    zero_planes(yb)
    zero_margins(hl0)
    zero_margins(hl1)
    sums[...] = jnp.zeros((LOCAL, 128), F32)

    def start(c, carry):
        x = pl.ds(2 + 2 * c, 2)
        value = yb[x] + 0.5 * (wf[pl.ds(2 * c, 2)] * ya[x])
        yb[x] = value
        put_halves(hl0, c, value)
        return carry

    for p in range(LOADS):
        loads[2 * p].wait()
        loads[2 * p + 1].wait()
        lax.fori_loop(p * XLOAD // 2, (p + 1) * XLOAD // 2, start, 0)
    run_chain(
        [
            ("middle", yb, ya, ya, wf, hl0, hl1, sums, None),
            ("middle", ya, yb, yb, wf, hl1, hl0, sums, None),
            ("last", yb, ya, ya, wf, hl0, None, sums, None),
        ],
        mats_ref,
    )
    stores = []
    if not final:
        stores.append(pltpu.make_async_copy(ya.at[pl.ds(2, G)], out_hbm, sem.at[0]))
        stores[-1].start()
    mean = jnp.sum(sums[...], axis=1, keepdims=True) * (1.0 / (G * PLANE))
    inverse = 1.0 / jnp.sqrt(mean + NORM_EPS)
    scale_ref[...] = jnp.broadcast_to(inverse, (LOCAL, 128))

    def finish(b, row, scale):
        slot = row if final else SLOTS - 1 - row
        for ref, half in ((dmine_ref, core), (dother_ref, 1 - core)):
            lane = cols(half * CELLS, CELLS)
            value = ya[2 + 16 * b + row, :, lane] * scale
            if final:
                yb[2 + 16 * b + row, :, lane] = value
            value = value * value
            value = value + pltpu.roll(value, 1, 0)
            value = value + pltpu.roll(value, 2, 0)
            for q in range(ROWS):
                ref[slot, pl.ds(b * ROWS + q, 1), :] = value[3:4, 128 * q : 128 * q + 128]
                ref[slot, pl.ds((FB + b) * ROWS + q, 1), :] = value[7:8, 128 * q : 128 * q + 128]
            if b == 0:
                ref[slot, pl.ds(PIECE, 2), :] = jnp.zeros((2, 128), F32)
        return scale

    scale = jnp.broadcast_to(inverse, (LOCAL, CELLS))
    for b in range(FB):
        scale = lax.fori_loop(0, SLOTS, functools.partial(finish, b), scale, unroll=4)
        if final:
            for o in range(LOCAL):
                stores.append(
                    pltpu.make_async_copy(
                        yb.at[pl.ds(2 + 16 * b, 16), o, :], out_hbm.at[o, pl.ds(16 * b, 16)], sem.at[b * LOCAL + o]
                    )
                )
                stores[-1].start()
    for store in stores:
        store.wait()


VMEM_SPEC = pl.BlockSpec(memory_space=pltpu.VMEM)
SMEM_SPEC = pl.BlockSpec(memory_space=pltpu.SMEM)
HBM_SPEC = pl.BlockSpec(memory_space=pltpu.HBM)
PLANES = pltpu.VMEM((G + 4, LOCAL, PLANE), F32)
RAW = jax.ShapeDtypeStruct((G, LOCAL, PLANE), F32)
RAW_HBM = pltpu.HBM((G, LOCAL, PLANE), F32)
SCALE = jax.ShapeDtypeStruct((LOCAL, 128), F32)
SPREAD = jax.ShapeDtypeStruct((SLOTS, PIECE + 2, 128), F32)
HALVES = pltpu.VMEM((2 * TILES, G * LOCAL, 128), BF16)


def in_hbm(value):
    return pltpu.with_memory_space_constraint(value, pltpu.HBM)


def prepare_call(first, source, mats):
    return pl.pallas_call(
        functools.partial(prepare_kernel, first),
        out_shape=(RAW_HBM, RAW_HBM),
        in_specs=[HBM_SPEC] + [VMEM_SPEC] * len(source),
        out_specs=(HBM_SPEC, HBM_SPEC),
        scratch_shapes=[PLANES, pltpu.VMEM(RAW.shape, F32), HALVES]
        + [pltpu.SemaphoreType.DMA((FB * (LOCAL + 1) + STEPS,))],
        name="prepare_first" if first else "prepare_next",
        cost_estimate=pl.CostEstimate(flops=2 * 10**9, bytes_accessed=11 * 10**6, transcendentals=0),
        compiler_params=pltpu.CompilerParams(vmem_limit_bytes=BIG),
    )(in_hbm(source[0]), *source[1:], mats)


def filter_call(final, field, plain, mine, other, mats):
    return pl.pallas_call(
        functools.partial(filter_kernel, final),
        out_shape=(pltpu.HBM((LOCAL, G, PLANE), F32) if final else RAW_HBM, SCALE, SPREAD, SPREAD),
        in_specs=[HBM_SPEC] * 2 + [VMEM_SPEC] * 3,
        out_specs=(HBM_SPEC,) + (VMEM_SPEC,) * 3,
        scratch_shapes=[
            PLANES,
            PLANES,
            pltpu.VMEM(RAW.shape, F32),
            HALVES,
            HALVES,
            pltpu.VMEM((LOCAL, 128), F32),
            pltpu.SemaphoreType.DMA((FB * LOCAL,)),
        ],
        name="filter_last" if final else "filter_first",
        cost_estimate=pl.CostEstimate(flops=8 * 10**9, bytes_accessed=14 * 10**6, transcendentals=0),
        compiler_params=pltpu.CompilerParams(vmem_limit_bytes=BIG),
    )(in_hbm(field), in_hbm(plain), mine, other, mats)


def entry(blocks_ref, group, e):
    return blocks_ref[e % FB, 2 * group + e // FB]


def select_kernel(count, blocks_ref, *refs):
    group = lax.axis_index("frag")
    ins, outs, rows = refs[:4], refs[4:-1], refs[-1]
    for k in range(count):
        for s in range(N_FRAG):
            for e in range(ENT):
                for q in range(ROWS):
                    rows[k, s * ENT + e, pl.ds(q, 1), :] = ins[s][k, pl.ds(e, 1), pl.ds(128 * q, 128)]
    for k in range(count):
        for e in range(ENT):
            block = entry(blocks_ref, group, e)
            place = lax.rem(group - block // ENT + N_FRAG, N_FRAG) * ENT + lax.rem(block, ENT)
            outs[k][pl.ds(e * ROWS, ROWS), :] = rows[k, place]
            outs[count + k][pl.ds(e * ROWS, ROWS), :] = rows[k, e]


def select_call(blocks, arrays):
    count = arrays[0].shape[0]
    piece = jax.ShapeDtypeStruct((PIECE, 128), F32)
    out_shape = (piece,) * (2 * count)
    return pl.pallas_call(
        functools.partial(select_kernel, count),
        out_shape=out_shape,
        in_specs=[SMEM_SPEC] + [VMEM_SPEC] * 4,
        out_specs=(VMEM_SPEC,) * (2 * count),
        scratch_shapes=[pltpu.VMEM((count, N_FRAG * ENT, ROWS, 128), F32)],
        name=f"select{count}",
        compiler_params=pltpu.CompilerParams(vmem_limit_bytes=8 << 20),
    )(blocks, *arrays)


def place_kernel(blocks_hbm, p0_hbm, p1, p2, p3, out_ref, rows, p0, blocks_ref, sem):
    loads = [pltpu.make_async_copy(blocks_hbm, blocks_ref, sem.at[0]), pltpu.make_async_copy(p0_hbm, p0, sem.at[1])]
    for load in loads:
        load.start()
    group = lax.axis_index("frag")
    for s, ref in ((1, p1), (2, p2), (3, p3), (0, p0)):
        if s == 0:
            for load in loads:
                load.wait()
        for e in range(ENT):
            for q in range(ROWS):
                rows[s * ENT + e, pl.ds(q, 1), :] = ref[pl.ds(e, 1), pl.ds(128 * q, 128)]
    tail = jnp.zeros((2, 128), F32)
    for e in range(ENT):
        block = entry(blocks_ref, group, e)
        place = lax.rem(group - block // ENT + N_FRAG, N_FRAG) * ENT + lax.rem(block, ENT)
        value = rows[place]
        for slot in range(SLOTS):
            out_ref[slot, pl.ds(e * ROWS, ROWS), :] = value
    for slot in range(SLOTS):
        out_ref[slot, pl.ds(PIECE, 2), :] = tail


def place_call(blocks, pots):
    return pl.pallas_call(
        place_kernel,
        out_shape=SPREAD,
        in_specs=[HBM_SPEC] * 2 + [VMEM_SPEC] * 3,
        out_specs=VMEM_SPEC,
        scratch_shapes=[
            pltpu.VMEM((N_FRAG * ENT, ROWS, 128), F32),
            pltpu.VMEM((ENT, CELLS), F32),
            pltpu.SMEM((FB, 2 * N_FRAG), jnp.int32),
            pltpu.SemaphoreType.DMA((2,)),
        ],
        name="place",
        compiler_params=pltpu.CompilerParams(vmem_limit_bytes=8 << 20),
    )(in_hbm(blocks), in_hbm(pots[0]), *pots[1:])


def update_kernel(final, blocks_ref, signs_ref, core_ref, ion_ref, d0, d1, d2, d3, out_ref):
    group = lax.axis_index("frag")
    seen = []
    for s, d in enumerate((d0, d1, d2, d3)):
        source = lax.rem(group - s + N_FRAG, N_FRAG)
        for k in range(ENT):
            sign = jnp.where(signs_ref[2 * source + k // FB] > 0, 1.0 / ORBS, -1.0 / ORBS)
            seen.append((entry(blocks_ref, source, k), sign.astype(F32), d[pl.ds(k * ROWS, ROWS), :]))
    for e in range(ENT):
        mine = group * ENT + e if final else entry(blocks_ref, group, e)
        total = core_ref[pl.ds(e * ROWS, ROWS), :]
        for block, sign, density in seen:
            total = total + jnp.where(block == mine, sign, jnp.float32(0.0)) * density
        total = jnp.maximum(total, DENSITY_FLOOR)
        root = jnp.exp(jnp.log(total) * (1.0 / 3.0))
        root = root - (root * root * root - total) / (3.0 * root * root)
        value = ion_ref[pl.ds(e * ROWS, ROWS), :] - EXCHANGE_COEF * root
        if final:
            for q in range(ROWS):
                out_ref[pl.ds(e, 1), pl.ds(128 * q, 128)] = value[q : q + 1]
        else:
            for slot in range(SLOTS):
                out_ref[slot, pl.ds(e * ROWS, ROWS), :] = value
    if not final:
        for slot in range(SLOTS):
            out_ref[slot, pl.ds(PIECE, 2), :] = jnp.zeros((2, 128), F32)


def update_call(final, blocks, signs, core, ion, densities):
    return pl.pallas_call(
        functools.partial(update_kernel, final),
        out_shape=jax.ShapeDtypeStruct((ENT, CELLS), F32) if final else SPREAD,
        in_specs=[SMEM_SPEC] * 2 + [VMEM_SPEC] * 6,
        out_specs=VMEM_SPEC,
        name="update_last" if final else "update_first",
        compiler_params=pltpu.CompilerParams(vmem_limit_bytes=8 << 20),
    )(blocks, signs, core, ion, *densities)


def frag_all(value):
    return [value] + [
        lax.ppermute(value, "frag", [(g, (g + s) % N_FRAG) for g in range(N_FRAG)]) for s in (1, 2, 3)
    ]


def core_swap(value):
    return lax.ppermute(value, "orb", [(i, i ^ 1) for i in range(2 * SLOTS)])


def plane_exchange(value, backward=False):
    order = range(SLOTS - 1, -1, -1) if backward else range(SLOTS)
    groups = [[2 * i + c for i in order] for c in range(2)]
    return lax.all_to_all(value, "orb", 0, 0, axis_index_groups=groups, tiled=True)


def shards(orbitals, potential, ion_potential, core_density, frag_blocks, frag_signs):
    blocks = frag_blocks.T
    mats = stencil_matrices().reshape(3, WIN, 2, 128).transpose(0, 2, 1, 3)
    mats = jnp.asarray(mats, BF16)

    pots = frag_all(potential)
    spread, source = lax.optimization_barrier((place_call(blocks, pots), orbitals.reshape(LOCAL, G, PLANE)))
    near = plane_exchange(spread)
    field, plain = prepare_call(True, (source,), mats)
    near, field = lax.optimization_barrier((near, field))
    statics = frag_all(jnp.stack([core_density, ion_potential]))
    raw, scale, mine, other = filter_call(False, field, plain, near, core_swap(near), mats)
    cores, ions, own_core, own_ion = select_call(blocks, statics)

    density = plane_exchange(mine + core_swap(other), backward=True)
    densities = frag_all(jnp.sum(density, axis=0))
    spread = update_call(False, blocks, frag_signs, cores, ions, densities)
    spread, raw = lax.optimization_barrier((spread, raw))
    near = plane_exchange(spread, backward=True)
    field, plain = prepare_call(False, (raw, scale), mats)
    near, field = lax.optimization_barrier((near, field))
    filtered, _, mine, other = filter_call(True, field, plain, near, core_swap(near), mats)
    density = plane_exchange(mine + core_swap(other))
    densities = frag_all(jnp.sum(density, axis=0))
    new_potential = update_call(True, blocks, frag_signs, own_core, own_ion, densities)
    return (filtered.reshape(orbitals.shape), new_potential)


def solution(mesh):
    in_specs = (
        P("frag", "orb", None, None),
        P("frag", "orb"),
        P("frag", "orb"),
        P("frag", "orb"),
        P(),
        P(),
    )
    out_specs = (P("frag", "orb", None, None), P("frag", "orb"))
    return jax.shard_map(shards, mesh=mesh, in_specs=in_specs, out_specs=out_specs, check_vma=False)
```

```python
import functools

import jax
import jax.numpy as jnp
import numpy as np
from jax import lax
from jax.experimental import pallas as pl
from jax.experimental.pallas import tpu as pltpu
from jax.sharding import PartitionSpec as P

G = 48
PLANE = G * G
FB = 3
ORBS = 128
N_FRAG = 4
SLOTS = 16
BAND = 64
BANDS = 6
UNROLL = 4
LOADS = 6
XLOAD = G // LOADS
BIG = 40 << 20
ENT = 6
CELLS = 1152
ROWS = CELLS // 128
PIECE = ENT * ROWS
LOCAL = 8
COLS = 256
WIN = 512
STEPS = PLANE // COLS
TILES = PLANE // 128 + 2
DENSITY_FLOOR = 0.25
EXCHANGE_COEF = 0.9847450218426965
NORM_EPS = 1e-6
F32 = jnp.float32
BF16 = jnp.bfloat16


def stencil_matrices():
    mats = np.zeros((3, WIN, COLS), np.float32)
    for phase in range(3):
        out = 768 + COLS * phase + np.arange(COLS)[None, :]
        src = 768 + COLS * phase - 128 + np.arange(WIN)[:, None]
        diff = np.abs(src - out)
        same = (src // G) == (out // G)
        mats[phase] = (
            np.where(diff == G, -16.0, 0.0)
            + np.where(diff == 2 * G, 1.0, 0.0)
            + np.where((diff == 1) & same, -16.0, 0.0)
            + np.where((diff == 2) & same, 1.0, 0.0)
        )
    return mats


def split(values):
    high = values.astype(BF16)
    low = (values - high.astype(F32)).astype(BF16)
    return high, low


def cols(start, size=128):
    return pl.ds(pl.multiple_of(start, 128), size)


def zero_planes(buf):
    buf[pl.ds(0, 2)] = jnp.zeros((2, LOCAL, PLANE), F32)
    buf[pl.ds(G + 2, 2)] = jnp.zeros((2, LOCAL, PLANE), F32)


def zero_margins(halves):
    for part in range(2):
        halves[part * TILES] = jnp.zeros((G * LOCAL, 128), BF16)
        halves[part * TILES + TILES - 1] = jnp.zeros((G * LOCAL, 128), BF16)


def put_halves(halves, c, values):
    rows = pl.ds(pl.multiple_of(16 * c, 16), 16)
    for j in range(TILES - 2):
        high, low = split(values[:, :, 128 * j : 128 * j + 128].reshape(16, 128))
        halves[1 + j, rows, :] = high
        halves[TILES + 1 + j, rows, :] = low


def run_chain(apps, mats_ref):
    def scoped(*accs):
        def acc(parity, unit, i):
            return accs[(2 * parity + unit) * BANDS + i]

        def push(n, parity, unit):
            mat = jnp.concatenate([mats_ref[lax.rem(n, 3), t, pl.ds(COLS * unit, COLS), :] for t in range(2)], axis=1)
            pltpu.matmul_push_rhs(mat, staging_register=parity, mxu_index=unit)

        def feed(app, n, parity, i):
            halves = app[5]
            rows = pl.ds(BAND * i, BAND)
            for unit in range(2):
                high, low = (
                    jnp.concatenate([halves[part * TILES + 2 * (n + unit) + t, rows, :] for t in range(2)], axis=1)
                    for part in range(2)
                )
                pltpu.matmul_acc_lhs(acc(parity, unit, i), high, load_staged_rhs=parity if i == 0 else None)
                pltpu.matmul_acc_lhs(acc(parity, unit, i), low)
                if i == BANDS - 2 + unit:
                    push(n + 1, 1 - parity, unit)

        def emit(app, n, parity, i):
            kind, cur, prev, dst, wf, _, halves_next, sums, done = app
            rows = pl.ds(BAND * i, BAND)
            values = pltpu.matmul_pop(acc(parity, 0, i)) + pltpu.matmul_pop(acc(parity, 1, i))
            for t in range(COLS // 128):
                lane = cols(COLS * n + 128 * t)
                near = cur[pl.ds(8 * i, 12), :, lane]
                s1 = near[1:9] + near[3:11]
                s2 = near[0:8] + near[4:12]
                plane = values[:, 128 * t : 128 * t + 128].reshape(8, LOCAL, 128)
                new = plane + s2 - 16.0 * s1
                here = pl.ds(8 * i + (0 if kind == "plain" else 2), 8)
                if kind == "plain":
                    dst[here, :, lane] = (0.5 / 48.0) * new
                    continue
                new = (1.0 / 48.0) * new + wf[pl.ds(8 * i, 8), :, lane] * near[2:10]
                new = new - prev[pl.ds(8 * i + 2, 8), :, lane]
                dst[here, :, lane] = new
                if kind == "last":
                    sums[...] += jnp.sum(new * new, axis=0)
                else:
                    high, low = split(new.reshape(BAND, 128))
                    halves_next[2 * n + t + 1, rows, :] = high
                    halves_next[TILES + 2 * n + t + 1, rows, :] = low
            if done is not None and i == BANDS - 1:
                done(n)

        for unit in range(2):
            push(0, 0, unit)
        for i in range(BANDS):
            feed(apps[0], 0, 0, i)
        for number, app in enumerate(apps):

            def body(j, carry):
                for u in range(UNROLL):
                    for i in range(BANDS):
                        feed(app, UNROLL * j + u + 1, (number + u + 1) % 2, i)
                        emit(app, UNROLL * j + u, (number + u) % 2, i)
                return carry

            lax.fori_loop(0, STEPS // UNROLL, body, 0)
            for i in range(BANDS):
                if number + 1 < len(apps):
                    feed(apps[number + 1], 0, (number + 1) % 2, i)
                emit(app, STEPS - 1, number % 2, i)
        rest = len(apps) % 2
        for unit in range(2):
            pltpu.matmul_acc_lhs(acc(rest, unit, 0), jnp.zeros((BAND, COLS), BF16), load_staged_rhs=rest)
            pltpu.matmul_pop(acc(rest, unit, 0))

    pl.run_scoped(
        scoped,
        *[pltpu.ACC(unit)((BAND, COLS), F32) for _ in range(2) for unit in range(2) for _ in range(BANDS)],
    )


def prepare_kernel(first, source, *refs):
    if first:
        mats_ref, field_hbm, plain_hbm, field, plain, hl, sem = refs
    else:
        scale_ref, mats_ref, field_hbm, plain_hbm, field, plain, hl, sem = refs
    loads = []
    for p in range(FB):
        inner = pl.ds(2 + 16 * p, 16)
        x = pl.ds(16 * p, 16)
        if first:
            loads.append(
                [
                    pltpu.make_async_copy(source.at[o, x], field.at[inner, o, :], sem.at[LOCAL * p + o])
                    for o in range(LOCAL)
                ]
            )
        else:
            loads.append([pltpu.make_async_copy(source.at[x], field.at[inner], sem.at[LOCAL * p])])
        for load in loads[-1]:
            load.start()
    zero_planes(field)
    zero_margins(hl)
    scale = None if first else jnp.broadcast_to(scale_ref[:, 0:1], (LOCAL, PLANE))

    def body(c, scale):
        x = pl.ds(2 + 2 * c, 2)
        values = field[x]
        if not first:
            values = values * scale[None]
            field[x] = values
        put_halves(hl, c, values)
        return scale

    stores = []
    for p in range(FB):
        for load in loads[p]:
            load.wait()
        lax.fori_loop(8 * p, 8 * p + 8, body, scale)
        stores.append(
            pltpu.make_async_copy(
                field.at[pl.ds(2 + 16 * p, 16)], field_hbm.at[pl.ds(16 * p, 16)], sem.at[FB * LOCAL + p]
            )
        )
        stores[-1].start()

    def column(n):
        lane = cols(COLS * n, COLS)
        return pltpu.make_async_copy(plain.at[:, :, lane], plain_hbm.at[:, :, lane], sem.at[FB * (LOCAL + 1) + n])

    run_chain([("plain", field, None, plain, None, hl, None, None, lambda n: column(n).start())], mats_ref)
    for store in stores:
        store.wait()
    for n in range(STEPS):
        column(n).wait()


def filter_kernel(final, field_hbm, plain_hbm, mine_ref, other_ref, mats_ref, out_hbm, scale_ref, dmine_ref,
                  dother_ref, ya, yb, wf, hl0, hl1, sums, sem):
    core = lax.axis_index("orb") % 2
    loads = []
    for p in range(LOADS):
        x = pl.ds(XLOAD * p, XLOAD)
        inner = pl.ds(2 + XLOAD * p, XLOAD)
        loads.append(pltpu.make_async_copy(field_hbm.at[x], ya.at[inner], sem.at[2 * p]))
        loads.append(pltpu.make_async_copy(plain_hbm.at[x], yb.at[inner], sem.at[2 * p + 1]))
    for load in loads:
        load.start()
    upper = lax.broadcasted_iota(jnp.int32, (LOCAL, 128), 0) >= LOCAL // 2

    def build(row, carry):
        slot = SLOTS - 1 - row
        for ref, half in ((mine_ref, core), (other_ref, 1 - core)):
            for b in range(FB):
                tiles = []
                for q in range(ROWS):
                    v0 = ref[slot, pl.ds(b * ROWS + q, 1), :]
                    v1 = ref[slot, pl.ds((FB + b) * ROWS + q, 1), :]
                    v = jnp.where(upper, jnp.broadcast_to(v1, (LOCAL, 128)), jnp.broadcast_to(v0, (LOCAL, 128)))
                    tiles.append(v * 0.125 - 0.375)
                wf[16 * b + row, :, cols(half * CELLS, CELLS)] = jnp.concatenate(tiles, axis=1)
        return carry

    lax.fori_loop(0, SLOTS, build, 0, unroll=2)
    zero_planes(ya)
    zero_planes(yb)
    zero_margins(hl0)
    zero_margins(hl1)
    sums[...] = jnp.zeros((LOCAL, 128), F32)

    def start(c, carry):
        x = pl.ds(2 + 2 * c, 2)
        value = yb[x] + 0.5 * (wf[pl.ds(2 * c, 2)] * ya[x])
        yb[x] = value
        put_halves(hl0, c, value)
        return carry

    for p in range(LOADS):
        loads[2 * p].wait()
        loads[2 * p + 1].wait()
        lax.fori_loop(p * XLOAD // 2, (p + 1) * XLOAD // 2, start, 0)
    run_chain(
        [
            ("middle", yb, ya, ya, wf, hl0, hl1, sums, None),
            ("middle", ya, yb, yb, wf, hl1, hl0, sums, None),
            ("last", yb, ya, ya, wf, hl0, None, sums, None),
        ],
        mats_ref,
    )
    stores = []
    if not final:
        stores.append(pltpu.make_async_copy(ya.at[pl.ds(2, G)], out_hbm, sem.at[0]))
        stores[-1].start()
    mean = jnp.sum(sums[...], axis=1, keepdims=True) * (1.0 / (G * PLANE))
    inverse = 1.0 / jnp.sqrt(mean + NORM_EPS)
    scale_ref[...] = jnp.broadcast_to(inverse, (LOCAL, 128))

    def finish(b, row, scale):
        slot = SLOTS - 1 - row
        for ref, half in ((dmine_ref, core), (dother_ref, 1 - core)):
            lane = cols(half * CELLS, CELLS)
            value = ya[2 + 16 * b + row, :, lane] * scale
            if final:
                yb[2 + 16 * b + row, :, lane] = value
            value = value * value
            value = value + pltpu.roll(value, 1, 0)
            value = value + pltpu.roll(value, 2, 0)
            for q in range(ROWS):
                ref[slot, pl.ds(b * ROWS + q, 1), :] = value[3:4, 128 * q : 128 * q + 128]
                ref[slot, pl.ds((FB + b) * ROWS + q, 1), :] = value[7:8, 128 * q : 128 * q + 128]
            if b == 0:
                ref[slot, pl.ds(PIECE, 2), :] = jnp.zeros((2, 128), F32)
        return scale

    scale = jnp.broadcast_to(inverse, (LOCAL, CELLS))
    for b in range(FB):
        scale = lax.fori_loop(0, SLOTS, functools.partial(finish, b), scale, unroll=4)
        if final:
            for o in range(LOCAL):
                stores.append(
                    pltpu.make_async_copy(
                        yb.at[pl.ds(2 + 16 * b, 16), o, :], out_hbm.at[o, pl.ds(16 * b, 16)], sem.at[b * LOCAL + o]
                    )
                )
                stores[-1].start()
    for store in stores:
        store.wait()


VMEM_SPEC = pl.BlockSpec(memory_space=pltpu.VMEM)
SMEM_SPEC = pl.BlockSpec(memory_space=pltpu.SMEM)
HBM_SPEC = pl.BlockSpec(memory_space=pltpu.HBM)
PLANES = pltpu.VMEM((G + 4, LOCAL, PLANE), F32)
RAW = jax.ShapeDtypeStruct((G, LOCAL, PLANE), F32)
RAW_HBM = pltpu.HBM((G, LOCAL, PLANE), F32)
SCALE = jax.ShapeDtypeStruct((LOCAL, 128), F32)
SPREAD = jax.ShapeDtypeStruct((SLOTS, PIECE + 2, 128), F32)
HALVES = pltpu.VMEM((2 * TILES, G * LOCAL, 128), BF16)


def in_hbm(value):
    return pltpu.with_memory_space_constraint(value, pltpu.HBM)


def prepare_call(first, source, mats):
    return pl.pallas_call(
        functools.partial(prepare_kernel, first),
        out_shape=(RAW_HBM, RAW_HBM),
        in_specs=[HBM_SPEC] + [VMEM_SPEC] * len(source),
        out_specs=(HBM_SPEC, HBM_SPEC),
        scratch_shapes=[PLANES, pltpu.VMEM(RAW.shape, F32), HALVES]
        + [pltpu.SemaphoreType.DMA((FB * (LOCAL + 1) + STEPS,))],
        name="prepare_first" if first else "prepare_next",
        cost_estimate=pl.CostEstimate(flops=2 * 10**9, bytes_accessed=11 * 10**6, transcendentals=0),
        compiler_params=pltpu.CompilerParams(vmem_limit_bytes=BIG),
    )(in_hbm(source[0]), *source[1:], mats)


def filter_call(final, field, plain, mine, other, mats):
    return pl.pallas_call(
        functools.partial(filter_kernel, final),
        out_shape=(pltpu.HBM((LOCAL, G, PLANE), F32) if final else RAW_HBM, SCALE, SPREAD, SPREAD),
        in_specs=[HBM_SPEC] * 2 + [VMEM_SPEC] * 3,
        out_specs=(HBM_SPEC,) + (VMEM_SPEC,) * 3,
        scratch_shapes=[
            PLANES,
            PLANES,
            pltpu.VMEM(RAW.shape, F32),
            HALVES,
            HALVES,
            pltpu.VMEM((LOCAL, 128), F32),
            pltpu.SemaphoreType.DMA((FB * LOCAL,)),
        ],
        name="filter_last" if final else "filter_first",
        cost_estimate=pl.CostEstimate(flops=8 * 10**9, bytes_accessed=14 * 10**6, transcendentals=0),
        compiler_params=pltpu.CompilerParams(vmem_limit_bytes=BIG),
    )(in_hbm(field), in_hbm(plain), mine, other, mats)


def entry(blocks_ref, group, e):
    return blocks_ref[e % FB, 2 * group + e // FB]


def select_kernel(count, blocks_ref, *refs):
    group = lax.axis_index("frag")
    ins, outs, rows = refs[:4], refs[4:-1], refs[-1]
    for k in range(count):
        for s in range(N_FRAG):
            for e in range(ENT):
                for q in range(ROWS):
                    rows[k, s * ENT + e, pl.ds(q, 1), :] = ins[s][k, pl.ds(e, 1), pl.ds(128 * q, 128)]
    for k in range(count):
        for e in range(ENT):
            block = entry(blocks_ref, group, e)
            place = lax.rem(group - block // ENT + N_FRAG, N_FRAG) * ENT + lax.rem(block, ENT)
            outs[k][pl.ds(e * ROWS, ROWS), :] = rows[k, place]
            outs[count + k][pl.ds(e * ROWS, ROWS), :] = rows[k, e]


def select_call(blocks, arrays):
    count = arrays[0].shape[0]
    piece = jax.ShapeDtypeStruct((PIECE, 128), F32)
    out_shape = (piece,) * (2 * count)
    return pl.pallas_call(
        functools.partial(select_kernel, count),
        out_shape=out_shape,
        in_specs=[SMEM_SPEC] + [VMEM_SPEC] * 4,
        out_specs=(VMEM_SPEC,) * (2 * count),
        scratch_shapes=[pltpu.VMEM((count, N_FRAG * ENT, ROWS, 128), F32)],
        name=f"select{count}",
        compiler_params=pltpu.CompilerParams(vmem_limit_bytes=8 << 20),
    )(blocks, *arrays)


def place_kernel(blocks_hbm, p0_hbm, p1, p2, p3, out_ref, rows, p0, blocks_ref, sem):
    loads = [pltpu.make_async_copy(blocks_hbm, blocks_ref, sem.at[0]), pltpu.make_async_copy(p0_hbm, p0, sem.at[1])]
    for load in loads:
        load.start()
    group = lax.axis_index("frag")
    for s, ref in ((1, p1), (2, p2), (3, p3), (0, p0)):
        if s == 0:
            for load in loads:
                load.wait()
        for e in range(ENT):
            for q in range(ROWS):
                rows[s * ENT + e, pl.ds(q, 1), :] = ref[pl.ds(e, 1), pl.ds(128 * q, 128)]
    tail = jnp.zeros((2, 128), F32)
    for e in range(ENT):
        block = entry(blocks_ref, group, e)
        place = lax.rem(group - block // ENT + N_FRAG, N_FRAG) * ENT + lax.rem(block, ENT)
        value = rows[place]
        for slot in range(SLOTS):
            out_ref[slot, pl.ds(e * ROWS, ROWS), :] = value
    for slot in range(SLOTS):
        out_ref[slot, pl.ds(PIECE, 2), :] = tail


def place_call(blocks, pots):
    return pl.pallas_call(
        place_kernel,
        out_shape=SPREAD,
        in_specs=[HBM_SPEC] * 2 + [VMEM_SPEC] * 3,
        out_specs=VMEM_SPEC,
        scratch_shapes=[
            pltpu.VMEM((N_FRAG * ENT, ROWS, 128), F32),
            pltpu.VMEM((ENT, CELLS), F32),
            pltpu.SMEM((FB, 2 * N_FRAG), jnp.int32),
            pltpu.SemaphoreType.DMA((2,)),
        ],
        name="place",
        compiler_params=pltpu.CompilerParams(vmem_limit_bytes=8 << 20),
    )(in_hbm(blocks), in_hbm(pots[0]), *pots[1:])


def update_kernel(final, blocks_ref, signs_ref, core_ref, ion_ref, d0, d1, d2, d3, out_ref):
    group = lax.axis_index("frag")
    seen = []
    for s, d in enumerate((d0, d1, d2, d3)):
        source = lax.rem(group - s + N_FRAG, N_FRAG)
        for k in range(ENT):
            sign = jnp.where(signs_ref[2 * source + k // FB] > 0, 1.0 / ORBS, -1.0 / ORBS)
            seen.append((entry(blocks_ref, source, k), sign.astype(F32), d[pl.ds(k * ROWS, ROWS), :]))
    for e in range(ENT):
        mine = group * ENT + e if final else entry(blocks_ref, group, e)
        total = core_ref[pl.ds(e * ROWS, ROWS), :]
        for block, sign, density in seen:
            total = total + jnp.where(block == mine, sign, jnp.float32(0.0)) * density
        total = jnp.maximum(total, DENSITY_FLOOR)
        root = jnp.exp(jnp.log(total) * (1.0 / 3.0))
        root = root - (root * root * root - total) / (3.0 * root * root)
        value = ion_ref[pl.ds(e * ROWS, ROWS), :] - EXCHANGE_COEF * root
        if final:
            for q in range(ROWS):
                out_ref[pl.ds(e, 1), pl.ds(128 * q, 128)] = value[q : q + 1]
        else:
            for slot in range(SLOTS):
                out_ref[slot, pl.ds(e * ROWS, ROWS), :] = value
    if not final:
        for slot in range(SLOTS):
            out_ref[slot, pl.ds(PIECE, 2), :] = jnp.zeros((2, 128), F32)


def update_call(final, blocks, signs, core, ion, densities):
    return pl.pallas_call(
        functools.partial(update_kernel, final),
        out_shape=jax.ShapeDtypeStruct((ENT, CELLS), F32) if final else SPREAD,
        in_specs=[SMEM_SPEC] * 2 + [VMEM_SPEC] * 6,
        out_specs=VMEM_SPEC,
        name="update_last" if final else "update_first",
        compiler_params=pltpu.CompilerParams(vmem_limit_bytes=8 << 20),
    )(blocks, signs, core, ion, *densities)


def frag_all(value):
    return [value] + [
        lax.ppermute(value, "frag", [(g, (g + s) % N_FRAG) for g in range(N_FRAG)]) for s in (1, 2, 3)
    ]


def core_swap(value):
    return lax.ppermute(value, "orb", [(i, i ^ 1) for i in range(2 * SLOTS)])


def plane_exchange(value):
    groups = [[2 * i + c for i in range(SLOTS - 1, -1, -1)] for c in range(2)]
    return lax.all_to_all(value, "orb", 0, 0, axis_index_groups=groups, tiled=True)


def shards(orbitals, potential, ion_potential, core_density, frag_blocks, frag_signs):
    blocks = frag_blocks.T
    mats = stencil_matrices().reshape(3, WIN, 2, 128).transpose(0, 2, 1, 3)
    mats = jnp.asarray(mats, BF16)

    pots = frag_all(potential)
    spread, source = lax.optimization_barrier((place_call(blocks, pots), orbitals.reshape(LOCAL, G, PLANE)))
    near = plane_exchange(spread)
    field, plain = prepare_call(True, (source,), mats)
    near, field = lax.optimization_barrier((near, field))
    statics = frag_all(jnp.stack([core_density, ion_potential]))
    raw, scale, mine, other = filter_call(False, field, plain, near, core_swap(near), mats)
    cores, ions, own_core, own_ion = select_call(blocks, statics)

    density = plane_exchange(mine + core_swap(other))
    densities = frag_all(jnp.sum(density, axis=0))
    spread = update_call(False, blocks, frag_signs, cores, ions, densities)
    spread, raw = lax.optimization_barrier((spread, raw))
    near = plane_exchange(spread)
    field, plain = prepare_call(False, (raw, scale), mats)
    near, field = lax.optimization_barrier((near, field))
    filtered, _, mine, other = filter_call(True, field, plain, near, core_swap(near), mats)
    density = plane_exchange(mine + core_swap(other))
    densities = frag_all(jnp.sum(density, axis=0))
    new_potential = update_call(True, blocks, frag_signs, own_core, own_ion, densities)
    return (filtered.reshape(orbitals.shape), new_potential)


def solution(mesh):
    in_specs = (
        P("frag", "orb", None, None),
        P("frag", "orb"),
        P("frag", "orb"),
        P("frag", "orb"),
        P(),
        P(),
    )
    out_specs = (P("frag", "orb", None, None), P("frag", "orb"))
    return jax.shard_map(shards, mesh=mesh, in_specs=in_specs, out_specs=out_specs, check_vma=False)
```
